256 devices in a mesh: grp: 2 (over y_lo), seq: 128 (over x, y_hi, z, core).
Axes of the slice: x: 4, y: 4 (y_hi: 2, y_lo: 2; y = y_hi * 2 + y_lo), z: 8, core: 2. Of those that a mesh axis runs over, the one named last changes fastest.
Arguments:
- q_inv: bfloat16 [4, 32768, 2048], P('grp', 'seq'), may hold values from -4.5 to 4.5
- k_inv: bfloat16 [4, 32768, 2048], P('grp', 'seq'), may hold values from -4.5 to 4.5
- v_inv: bfloat16 [4, 32768, 2048], P('grp', 'seq'), may hold values from -6 to 6
- group_ids: int32 [4], replicated, may hold values from 0 to 3, each once
- w_attr: bfloat16 [4, 2048, 64], replicated, may hold values from -2.390625 to 2.390625
- env_ids: int32 [4, 32768], P('grp', 'seq'), may hold values from 0 to 4095
- env_table: bfloat16 [4096, 128], replicated, may hold values from -6 to 6
- w_embed_attr: bfloat16 [4, 64, 4096], replicated, may hold values from -1.5 to 1.5
- w_embed_env: bfloat16 [128, 4096], replicated, may hold values from -1.5 to 1.5
- mod_scale: bfloat16 [4, 4096], P('grp'), may hold values from -3 to 3
- mod_shift: bfloat16 [4, 4096], P('grp'), may hold values from -3 to 3
- w_final: bfloat16 [4096, 64], replicated, may hold values from -0.09375 to 0.09375
Outputs:
- attributes: bfloat16 [4, 32768, 64], P('grp', 'seq')
- rendered: bfloat16 [4, 32768, 64], P('grp', 'seq')
The draws below stay inside these ranges and needn't reach their ends.
Inputs may be any that keep to these rules, and one draw needn't show every extreme that they name: `group_ids`: each kind 0 to 3 appears once.
All inputs are finite; a program needn't handle non-finite values.
Results may differ from the reference program's by a relative error of at most 0.012.
Values may be sent and summed in bfloat16 or wider, within the bound.
No kernel may reach another device: no remote copies, remote signals or barrier semaphores. Data moves between devices by JAX's collectives and lax.ppermute only.
A program may use at most 128 MiB of HBM per device.

```python
import math
import jax
import jax.numpy as jnp
import numpy as np
from jax import lax

D = 4096
HEADS = 16
HD = 128
HW = 2048
PATCH = 64
KINDS = 4
LIGHTS = 4
ENV_CH = 128
ENV_VOCAB = 4096
TOKENS = 32768
SEQ_LEN = 1024


def draw_q_inv(key, part):
    array_shape = (KINDS, TOKENS, HEADS * HD)
    values = jnp.clip(jax.random.normal(jax.random.fold_in(key, 1), array_shape, jnp.float32), -4.5, 4.5)
    return values.astype(jnp.bfloat16)


def draw_k_inv(key, part):
    array_shape = (KINDS, TOKENS, HEADS * HD)
    values = jnp.clip(jax.random.normal(jax.random.fold_in(key, 2), array_shape, jnp.float32), -4.5, 4.5)
    return values.astype(jnp.bfloat16)


def column_scale(key):
    return jnp.exp(jax.random.uniform(jax.random.fold_in(key, 21), (D,), jnp.float32, 0.0, math.log(10.0)))


def embed_weight(key, salt, array_shape):
    entries = jnp.clip(jax.random.normal(jax.random.fold_in(key, salt), array_shape, jnp.float32), -3.0, 3.0)
    return (entries * column_scale(key) * 0.05).astype(jnp.bfloat16)


def draw_w_embed_attr(key, part):
    return embed_weight(key, 22, (KINDS, PATCH, D))


def draw_w_embed_env(key, part):
    return embed_weight(key, 23, (ENV_CH, D))


def with_ends(array, stream_key, low, largest):
    extent = array.shape
    index_at = [jax.random.randint(jax.random.fold_in(stream_key, axis), (), 0, extent[axis]) for axis in range(len(extent))]
    array = array.at[tuple(index_at)].set(low)
    longest = extent.index(max(extent))
    index_at[longest] = (index_at[longest] + 1) % extent[longest]
    return array.at[tuple(index_at)].set(largest)


def level_of(rng, shape, shards, low, largest):
    loudness, own = 1.0, jax.random.fold_in(rng, 6)
    for position, blocks in shards:
        draws = jnp.exp(jax.random.uniform(jax.random.fold_in(own, position), (blocks,), jnp.float32, low / len(shards), largest / len(shards)))
        loudness = loudness * jnp.repeat(draws, shape[position] // blocks).reshape([-1 if axis == position else 1 for axis in range(len(shape))])
    return loudness


def rank_bounds(number_of, slope):
    portions = [(1 << 20) // math.isqrt(rank ** slope) + 1 for rank in range(1, number_of + 1)]
    scale = 1 + sum(portions) // (1 << 30)
    return np.cumsum(np.array([max(1, weight // scale) for weight in portions]))


def ranked(stream_key, dims, count, skew):
    table = rank_bounds(count, skew)
    pick = jax.random.randint(jax.random.fold_in(stream_key, 1), dims, 0, int(table[count - 1]))
    rank = jnp.searchsorted(jnp.asarray(table, jnp.int32), pick, side="right")
    return jax.random.permutation(jax.random.fold_in(stream_key, 2), count)[rank].astype(jnp.int32)


def gaussian(stream_key, extent, scale, reach, split=(), dtype=jnp.bfloat16):
    level = level_of(stream_key, extent, split, -0.22, 0.18) if split else 1.0
    array = jax.random.normal(stream_key, extent, jnp.float32) * scale * level
    return jnp.minimum(jnp.maximum(array, -reach), reach).astype(dtype)


def setup_inputs(seed: int = 0) -> dict:
    splits = jax.random.split(jax.random.key(seed), 13)
    q_inv = draw_q_inv(jax.random.fold_in(splits[12], 71), 0)
    k_inv = draw_k_inv(jax.random.fold_in(splits[12], 71), 0)
    v_inv = gaussian(splits[2], (KINDS, TOKENS, HW), 1.0, 6.0, ((0, 2), (1, 128)))
    group_ids = jax.random.permutation(splits[3], KINDS).astype(jnp.int32)
    w_attr = gaussian(splits[4], (KINDS, HW, PATCH), 0.4, 2.390625)
    env_ids = with_ends(ranked(splits[5], (LIGHTS, TOKENS), ENV_VOCAB, 2), jax.random.fold_in(splits[5], 3), 0, ENV_VOCAB - 1).astype(jnp.int32)
    env_table = gaussian(splits[6], (ENV_VOCAB, ENV_CH), 1.0, 6.0)
    w_embed_attr = draw_w_embed_attr(jax.random.fold_in(splits[12], 71), 0)
    w_embed_env = draw_w_embed_env(jax.random.fold_in(splits[12], 71), 0)
    mod_scale = gaussian(splits[9], (LIGHTS, D), 0.5, 3.0, ((0, 2),))
    mod_shift = gaussian(splits[10], (LIGHTS, D), 0.5, 3.0, ((0, 2),))
    w_final = gaussian(splits[11], (D, PATCH), D ** -0.5, 0.09375)
    return dict(q_inv=q_inv, k_inv=k_inv, v_inv=v_inv, group_ids=group_ids, w_attr=w_attr, env_ids=env_ids, env_table=env_table, w_embed_attr=w_embed_attr, w_embed_env=w_embed_env, mod_scale=mod_scale, mod_shift=mod_shift, w_final=w_final)


def attend_one(queries, keys_in, values_in):
    query_heads = queries.reshape(SEQ_LEN, HEADS, HD).astype(jnp.float32)
    key_heads = keys_in.reshape(SEQ_LEN, HEADS, HD).astype(jnp.float32)
    value_heads = values_in.reshape(SEQ_LEN, HEADS, HD).astype(jnp.float32)
    scores = jnp.einsum('qhd,khd->hqk', query_heads, key_heads) * HD ** (-0.5)
    row_max = lax.optimization_barrier(jnp.max(scores, axis=-1, keepdims=True))
    powers = jnp.exp(scores - row_max)
    totals = lax.optimization_barrier(jnp.sum(powers, axis=-1))
    weights = lax.optimization_barrier(powers.astype(jnp.bfloat16)).astype(jnp.float32)
    summed = jnp.einsum('hqk,khd->hqd', weights, value_heads) / totals[..., None]
    return jnp.transpose(summed, (1, 0, 2)).reshape(SEQ_LEN, HEADS * HD).astype(jnp.bfloat16)

def reference(q_inv, k_inv, v_inv, group_ids, w_attr, env_ids, env_table, w_embed_attr, w_embed_env, mod_scale, mod_shift, w_final):
    seq_count = TOKENS // SEQ_LEN
    width_all = HEADS * HD
    query_blocks = q_inv.reshape(KINDS * seq_count, SEQ_LEN, width_all)
    key_blocks = k_inv.reshape(KINDS * seq_count, SEQ_LEN, width_all)
    value_blocks = v_inv.reshape(KINDS * seq_count, SEQ_LEN, width_all)
    attended = lax.map(lambda triple: attend_one(triple[0], triple[1], triple[2]), (query_blocks, key_blocks, value_blocks))
    attended = attended.reshape(KINDS, TOKENS, width_all)
    readouts = []
    for group in range(KINDS):
        weight = w_attr[group_ids[group]]
        readouts.append(jnp.dot(attended[group], weight, preferred_element_type=jnp.float32).astype(jnp.bfloat16))
    attributes = jnp.stack(readouts)
    embedded = jnp.zeros((TOKENS, D), jnp.float32)
    for group in range(KINDS):
        embedded = embedded + jnp.dot(attributes[group], w_embed_attr[group_ids[group]], preferred_element_type=jnp.float32)
    rendered = []
    for light in range(LIGHTS):
        lighting = env_table[env_ids[light]]
        state = embedded + jnp.dot(lighting, w_embed_env, preferred_element_type=jnp.float32)
        average = lax.optimization_barrier(jnp.mean(state, axis=-1, keepdims=True))
        centred = state - average
        spread = lax.optimization_barrier(jnp.mean(centred * centred, axis=-1, keepdims=True))
        normed = centred / jnp.sqrt(spread + 1e-06)
        modulated = normed * (1.0 + mod_scale[light].astype(jnp.float32)) + mod_shift[light].astype(jnp.float32)
        modulated = modulated.astype(jnp.bfloat16)
        rendered.append(jnp.dot(modulated, w_final, preferred_element_type=jnp.float32).astype(jnp.bfloat16))
    return (attributes, jnp.stack(rendered))
```

```python
import math

import jax
import jax.numpy as jnp
from jax import lax
from jax.experimental import pallas as pl
from jax.experimental.pallas import tpu as pltpu
from jax.sharding import PartitionSpec as P

HD = 128
PARTS = 2
STEP_HEADS = 2
TILE = 512
EPS = 1e-06
SCALE = HD ** (-0.5) * math.log2(math.e)


def seq_swap(block, flip):
    count = lax.axis_size("seq")
    return lax.ppermute(block, "seq", [(i, i ^ flip) for i in range(count)])


def grp_swap(block):
    return lax.ppermute(block, "grp", [(0, 1), (1, 0)])


def both_swap(block):
    count = lax.axis_size("seq")
    route = [
        (g * count + i, (1 - g) * count + (i ^ 1)) for g in range(2) for i in range(count)
    ]
    return lax.ppermute(block, ("grp", "seq"), route)


def head_scores(keys, queries, values):
    scores = lax.dot_general(
        keys, queries, (((1,), (1,)), ((), ())), preferred_element_type=jnp.float32
    )
    top = jnp.max(scores, axis=0, keepdims=True)
    powers = jnp.exp2((scores - top) * SCALE).astype(jnp.bfloat16)
    summed = jnp.dot(values, powers, preferred_element_type=jnp.float32)
    return summed, top * SCALE


def local_kernel(ids, q, qx, k, kx, v, vx, w, vw, mean, level):
    step = pl.program_id(0)
    rows = q.shape[0]
    part = rows // PARTS
    for i in range(STEP_HEADS):
        cols = slice(i * HD, (i + 1) * HD)
        keys = jnp.concatenate((k[:, cols], kx[:, cols]), axis=0)
        values = jnp.concatenate((v[:, cols], vx[:, cols]), axis=0)
        read = lax.dot_general(
            w[cols, :], values, (((0,), (1,)), ((), ())), preferred_element_type=jnp.float32
        )
        read = jnp.concatenate(
            (read.astype(jnp.bfloat16), jnp.ones((16, read.shape[1]), jnp.bfloat16)), axis=0
        )
        vw[i] = read
        for j in range(PARTS):
            span = slice(j * part, (j + 1) * part)
            queries = jnp.concatenate((q[span, cols], qx[span, cols]), axis=0)
            summed, top = head_scores(keys, queries, read)
            total = summed[64:65]
            mean[j, i] = summed[:64] * (1.0 / total)
            level[j, pl.ds(step * STEP_HEADS + i, 1), :] = top + jnp.log2(total)


def remote_kernel(ids, qs, qd, k, kx, vw, home, out, acc, share):
    step = pl.program_id(0)

    @pl.when(step == 0)
    def _():
        acc[...] = jnp.zeros_like(acc)

    gathered = acc[...]
    for i in range(STEP_HEADS):
        cols = slice(i * HD, (i + 1) * HD)
        keys = jnp.concatenate((k[:, cols], kx[:, cols]), axis=0)
        queries = jnp.concatenate((qs[:, cols], qd[:, cols]), axis=0)
        summed, top = head_scores(keys, queries, vw[i])
        total = summed[64:65]
        row = pl.ds(step * STEP_HEADS + i, 1)
        mine = 1.0 / (1.0 + jnp.exp2(home[row, :] - (top + jnp.log2(total))))
        mine = mine.astype(jnp.bfloat16).astype(jnp.float32)
        share[row, :] = mine
        gathered = gathered + summed[:64] * (mine / total)
    acc[...] = gathered

    @pl.when(step == pl.num_programs(0) - 1)
    def _():
        out[:64] = acc[...].astype(jnp.bfloat16)
        out[64:] = share[...].astype(jnp.bfloat16)


def merge_kernel(remote, mean, own, other):
    acc = remote[:64].astype(jnp.float32)
    for h in range(mean.shape[0]):
        keep = 1.0 - remote[64 + h : 65 + h].astype(jnp.float32)
        acc = acc + mean[h] * keep
    acc = acc.astype(jnp.bfloat16)
    half = acc.shape[1] // 2
    own[...] = acc[:, :half]
    other[...] = acc[:, half:]


def render_kernel(
    ids, a0, a1, a2, a3, w0, w1, w2, w3, light, w_env, scale, shift, w_final, attrs, rendered, state
):
    lights, rows, width = state.shape
    me = ids[0]
    first = a0[...].astype(jnp.float32).T.astype(jnp.bfloat16)
    second = a1[...].astype(jnp.float32).T.astype(jnp.bfloat16)
    attrs[pl.ds(me, 1)] = first[None]
    attrs[pl.ds(1 - me, 1)] = second[None]
    latents = jnp.concatenate((a0[...], a1[...], a2[...], a3[...]), axis=0)
    latents = latents.astype(jnp.float32).T.astype(jnp.bfloat16)
    sums = [jnp.zeros((rows, 128), jnp.float32) for _ in range(lights)]

    def fold(block):
        total = block[:, :128]
        for s in range(1, block.shape[1] // 128):
            total = total + block[:, s * 128 : (s + 1) * 128]
        return total

    for t in range(width // TILE):
        cols = slice(t * TILE, (t + 1) * TILE)
        weight = jnp.concatenate((w0[:, cols], w1[:, cols], w2[:, cols], w3[:, cols]), axis=0)
        embedded = jnp.dot(latents, weight, preferred_element_type=jnp.float32)
        for l in range(lights):
            block = embedded + jnp.dot(
                light[l], w_env[:, cols], preferred_element_type=jnp.float32
            )
            state[l, :, cols] = block
            sums[l] = sums[l] + fold(block)
    for l in range(lights):
        average = jnp.sum(sums[l], axis=1, keepdims=True) * (1.0 / width)
        square = jnp.zeros((rows, 128), jnp.float32)
        for t in range(width // TILE):
            cols = slice(t * TILE, (t + 1) * TILE)
            centred = state[l, :, cols] - average
            square = square + fold(centred * centred)
        spread = jnp.sum(square, axis=1, keepdims=True) * (1.0 / width)
        invert = lax.rsqrt(spread + EPS)
        acc = jnp.zeros((rows, w_final.shape[1]), jnp.float32)
        for t in range(width // TILE):
            cols = slice(t * TILE, (t + 1) * TILE)
            gain = 1.0 + scale[l : l + 1, cols].astype(jnp.float32)
            bias = shift[l : l + 1, cols].astype(jnp.float32)
            normed = (state[l, :, cols] - average) * invert
            modulated = (normed * gain + bias).astype(jnp.bfloat16)
            acc = acc + jnp.dot(modulated, w_final[cols, :], preferred_element_type=jnp.float32)
        rendered[l] = acc.astype(jnp.bfloat16)


def whole(shape):
    return pl.BlockSpec(shape, lambda *_: (0,) * len(shape))


def on_device(
    q_inv,
    k_inv,
    v_inv,
    group_ids,
    w_attr,
    env_ids,
    env_table,
    w_embed_attr,
    w_embed_env,
    mod_scale,
    mod_shift,
    w_final,
):
    groups, rows, width = q_inv.shape
    heads = width // HD
    part = rows // PARTS
    wide = 2 * part
    patch = w_attr.shape[2]
    me = lax.axis_index("seq") % 2
    grp = lax.axis_index("grp")
    mine = 2 * grp + me
    others = jnp.stack((mine, 2 * grp + 1 - me, 2 * (1 - grp) + me, 2 * (1 - grp) + 1 - me))
    kinds = group_ids[others]
    ids = jnp.concatenate((me[None], kinds)).astype(jnp.int32)

    def pick(array, group, start=0, count=rows):
        return lax.dynamic_slice(array, (group, start, 0), (1, count, width))[0]

    same, cross = [], []
    for j in range(PARTS):
        same.append(seq_swap(pick(q_inv, me, j * part, part), 2))
        cross.append(seq_swap(pick(q_inv, 1 - me, j * part, part), 3))
    kx = seq_swap(pick(k_inv, 1 - me), 1)
    vx = seq_swap(pick(v_inv, 1 - me), 1)
    qx = seq_swap(pick(q_inv, 1 - me), 1)

    cols = STEP_HEADS * HD
    steps = heads // STEP_HEADS
    picked = pl.BlockSpec((None, rows, cols), lambda g, s: (s[0], 0, g))
    plain = pl.BlockSpec((rows, cols), lambda g, s: (0, g))
    vw, mean, level = pl.pallas_call(
        local_kernel,
        grid_spec=pltpu.PrefetchScalarGridSpec(
            num_scalar_prefetch=1,
            grid=(steps,),
            in_specs=[
                picked,
                plain,
                picked,
                plain,
                picked,
                plain,
                pl.BlockSpec((None, cols, patch), lambda g, s: (s[1], g, 0)),
            ],
            out_specs=[
                pl.BlockSpec((STEP_HEADS, 80, 2 * rows), lambda g, s: (g, 0, 0)),
                pl.BlockSpec((PARTS, STEP_HEADS, 64, wide), lambda g, s: (0, g, 0, 0)),
                whole((PARTS, heads, wide)),
            ],
        ),
        out_shape=[
            jax.ShapeDtypeStruct((heads, 80, 2 * rows), jnp.bfloat16),
            jax.ShapeDtypeStruct((PARTS, heads, 64, wide), jnp.float32),
            jax.ShapeDtypeStruct((PARTS, heads, wide), jnp.float32),
        ],
        name="local",
    )(ids, q_inv, qx, k_inv, kx, v_inv, vx, w_attr)
    home = seq_swap(level, 2)
    lighting = jnp.take(env_table, env_ids, axis=0)

    remote = []
    for j in range(PARTS):
        block = pl.BlockSpec((part, cols), lambda g, s: (0, g))
        sent = pl.pallas_call(
            remote_kernel,
            grid_spec=pltpu.PrefetchScalarGridSpec(
                num_scalar_prefetch=1,
                grid=(steps,),
                in_specs=[
                    block,
                    block,
                    picked,
                    plain,
                    pl.BlockSpec((STEP_HEADS, 80, 2 * rows), lambda g, s: (g, 0, 0)),
                    pl.BlockSpec((None, heads, wide), lambda g, s, j=j: (j, 0, 0)),
                ],
                out_specs=whole((64 + heads, wide)),
                scratch_shapes=[
                    pltpu.VMEM((64, wide), jnp.float32),
                    pltpu.VMEM((heads, wide), jnp.float32),
                ],
            ),
            out_shape=jax.ShapeDtypeStruct((64 + heads, wide), jnp.bfloat16),
            name="remote",
        )(ids, same[j], cross[j], k_inv, kx, vw, home)
        remote.append(seq_swap(sent, 2))

    attrs, renders = [], []
    lights = mod_scale.shape[0]
    model = w_final.shape[0]
    channels = w_embed_env.shape[0]
    for j in range(PARTS):
        own, other = pl.pallas_call(
            merge_kernel,
            grid=(1,),
            in_specs=[
                whole((64 + heads, wide)),
                pl.BlockSpec((None, heads, 64, wide), lambda g, j=j: (j, 0, 0, 0)),
            ],
            out_specs=[whole((64, part)), whole((64, part))],
            out_shape=[jax.ShapeDtypeStruct((64, part), jnp.bfloat16)] * 2,
            name="merge",
        )(remote[j], mean)
        a1 = seq_swap(other, 1)
        a2 = grp_swap(own)
        a3 = both_swap(other)
        weights = [
            pl.BlockSpec((None, patch, model), lambda g, s, n=n: (s[1 + n], 0, 0))
            for n in range(4)
        ]
        attr, render = pl.pallas_call(
            render_kernel,
            grid_spec=pltpu.PrefetchScalarGridSpec(
                num_scalar_prefetch=1,
                grid=(1,),
                in_specs=[whole((64, part))] * 4
                + weights
                + [
                    pl.BlockSpec((lights, part, channels), lambda g, s, j=j: (0, j, 0)),
                    whole((channels, model)),
                    whole((lights, model)),
                    whole((lights, model)),
                    whole((model, patch)),
                ],
                out_specs=[whole((groups, part, patch)), whole((lights, part, patch))],
                scratch_shapes=[pltpu.VMEM((lights, part, model), jnp.float32)],
            ),
            out_shape=[
                jax.ShapeDtypeStruct((groups, part, patch), jnp.bfloat16),
                jax.ShapeDtypeStruct((lights, part, patch), jnp.bfloat16),
            ],
            name="render",
        )(
            ids,
            own,
            a1,
            a2,
            a3,
            w_embed_attr,
            w_embed_attr,
            w_embed_attr,
            w_embed_attr,
            lighting,
            w_embed_env,
            mod_scale,
            mod_shift,
            w_final,
        )
        attrs.append(attr)
        renders.append(render)
    return (jnp.concatenate(attrs, axis=1), jnp.concatenate(renders, axis=1))


def solution(mesh):
    in_specs = (
        P("grp", "seq", None),
        P("grp", "seq", None),
        P("grp", "seq", None),
        P(),
        P(),
        P("grp", "seq"),
        P(),
        P(),
        P(),
        P("grp", None),
        P("grp", None),
        P(),
    )
    out_specs = (P("grp", "seq", None), P("grp", "seq", None))
    return jax.shard_map(
        on_device, mesh=mesh, in_specs=in_specs, out_specs=out_specs, check_vma=False
    )
```

```python
import math

import jax
import jax.numpy as jnp
from jax import lax
from jax.experimental import pallas as pl
from jax.experimental.pallas import tpu as pltpu
from jax.sharding import PartitionSpec as P


HD = 128
STEP_HEADS = 4
EPS = 1e-06
SCALE = HD ** (-0.5) * math.log2(math.e)
SAFE = 60.0
CHUNK = 1024
OVER_LANES = (((1,), (1,)), ((), ()))


def seq_swap(block, flip):
    count = lax.axis_size("seq")
    return lax.ppermute(block, "seq", [(i, i ^ flip) for i in range(count)])


def grp_swap(block):
    return lax.ppermute(block, "grp", [(0, 1), (1, 0)])


def both_swap(block):
    count = lax.axis_size("seq")
    route = [
        (g * count + i, (1 - g) * count + (i ^ 1)) for g in range(2) for i in range(count)
    ]
    return lax.ppermute(block, ("grp", "seq"), route)


def dot_lanes(left, right):
    return lax.dot_general(left, right, OVER_LANES, preferred_element_type=jnp.float32)


def split(block):
    high = block.astype(jnp.bfloat16)
    return high, (block - high.astype(jnp.float32)).astype(jnp.bfloat16)


def dot_split(left, right):
    high, low = split(left)
    return dot_lanes(high, right) + dot_lanes(low, right)


def plain_softmax(keys, queries, values):
    powers = jnp.exp2(dot_lanes(keys, queries) * SCALE).astype(jnp.bfloat16)
    summed = jnp.dot(values, powers, preferred_element_type=jnp.float32)
    total = summed[64:65]
    return summed[:64], total, jnp.log2(total)


def shifted_softmax(keys, queries, values):
    scores = dot_lanes(keys, queries)
    top = jnp.max(scores, axis=0, keepdims=True)
    powers = jnp.exp2((scores - top) * SCALE).astype(jnp.bfloat16)
    summed = jnp.dot(values, powers, preferred_element_type=jnp.float32)
    total = summed[64:65]
    return summed[:64], total, top * SCALE + jnp.log2(total)


def worst(levels):
    largest = jnp.abs(levels[0])
    for level in levels[1:]:
        largest = jnp.maximum(largest, jnp.abs(level))
    return jnp.max(largest)


def local_kernel(ids, q, qx, k, kx, v, vx, w, vw, mean, level):
    step = pl.program_id(0)

    for i in range(STEP_HEADS):
        cols = slice(i * HD, (i + 1) * HD)
        values = jnp.concatenate((v[:, cols], vx[:, cols]), axis=0)
        read = dot_lanes(w[:, cols], values).astype(jnp.bfloat16)
        vw[i, :64] = read
        vw[i, 64:] = jnp.ones((16, read.shape[1]), jnp.bfloat16)

    def attend(softmax):
        levels = []
        for i in range(STEP_HEADS):
            cols = slice(i * HD, (i + 1) * HD)
            keys = jnp.concatenate((k[:, cols], kx[:, cols]), axis=0)
            rows = []
            for lanes, spans in ((0, ((0, 128),)), (256, ((128, 192), (192, 256)))):
                pieces = []
                for a, b in spans:
                    pieces += [q[a:b, cols], qx[a:b, cols]]
                summed, total, row = softmax(keys, jnp.concatenate(pieces, axis=0), vw[i])
                mean[i, :, lanes : lanes + 256] = summed * (1.0 / total)
                rows.append(row)
            row = jnp.concatenate(rows, axis=1)
            level[pl.ds(step * STEP_HEADS + i, 1), :] = row
            levels.append(row)
        return worst(levels)

    reach = attend(plain_softmax)

    @pl.when(jnp.logical_not(reach < SAFE))
    def _():
        attend(shifted_softmax)


def remote_kernel(spans, ids, qs, qd, k, kx, vw, home, out, acc, share):
    step = pl.program_id(0)

    @pl.when(step == 0)
    def _():
        acc[...] = jnp.zeros_like(acc)

    before = acc[...]

    def attend(softmax):
        gathered = [before[:, a * 2 : b * 2] for a, b in spans]
        levels = []
        for i in range(STEP_HEADS):
            cols = slice(i * HD, (i + 1) * HD)
            keys = jnp.concatenate((k[:, cols], kx[:, cols]), axis=0)
            row = pl.ds(step * STEP_HEADS + i, 1)
            theirs = home[row, :]
            rows, mines = [], []
            for n, (a, b) in enumerate(spans):
                queries = jnp.concatenate((qs[a:b, cols], qd[a:b, cols]), axis=0)
                summed, total, level = softmax(keys, queries, vw[i])
                mine = 1.0 / (1.0 + jnp.exp2(theirs[:, 2 * a : 2 * b] - level))
                mine = mine.astype(jnp.bfloat16).astype(jnp.float32)
                gathered[n] = gathered[n] + summed * (mine / total)
                mines.append(mine)
                rows.append(level)
            share[row, :] = jnp.concatenate(mines, axis=1)
            levels.append(jnp.concatenate(rows, axis=1))
        for n, (a, b) in enumerate(spans):
            acc[:, 2 * a : 2 * b] = gathered[n]
        return worst(levels)

    reach = attend(plain_softmax)

    @pl.when(jnp.logical_not(reach < SAFE))
    def _():
        attend(shifted_softmax)

    @pl.when(step == pl.num_programs(0) - 1)
    def _():
        out[:64] = acc[...].astype(jnp.bfloat16)
        out[64:] = share[...].astype(jnp.bfloat16)


def blend(remote, mean, start):
    acc = remote[:64].astype(jnp.float32)
    for h in range(mean.shape[0]):
        keep = 1.0 - remote[64 + h : 65 + h].astype(jnp.float32)
        acc = acc + mean[h, :, start : start + acc.shape[1]] * keep
    return acc


def early_kernel(remote, mean, out):
    out[...] = blend(remote, mean, 0)


def merge_kernel(remote, mean, early, own, other):
    late = blend(remote, mean, early.shape[1])
    mixed = early[:, 256:]
    first = lax.broadcasted_iota(jnp.int32, late.shape, 1) < 64
    own[:, :128] = early[:, :128].astype(jnp.bfloat16)
    other[:, :128] = early[:, 128:256].astype(jnp.bfloat16)
    own[:, 128:] = jnp.where(first, mixed, pltpu.roll(late, 64, 1)).astype(jnp.bfloat16)
    other[:, 128:] = jnp.where(first, pltpu.roll(mixed, 64, 1), late).astype(jnp.bfloat16)


def prepare_kernel(
    ids, w0, w1, w2, w3, w_env, final, scale, shift, light,
    mixer, cross, direct, base, bias, reads, gram, column, sums, shifts,
):
    step = pl.program_id(0)
    lights = scale.shape[0]
    width = pl.num_programs(0) * w0.shape[1]

    @pl.when(step == 0)
    def _():
        for ref in (reads, gram, column, sums, shifts):
            ref[...] = jnp.zeros_like(ref)

    rows = jnp.concatenate((w0[...], w1[...], w2[...], w3[...], w_env[...]), axis=0)
    weight = final[...].astype(jnp.float32)

    def fold(block):
        total = block[:, :128]
        for s in range(1, block.shape[1] // 128):
            total = total + block[:, s * 128 : (s + 1) * 128]
        return total

    gains = []
    for l in range(lights):
        gained = weight * (1.0 + scale[l : l + 1, :].astype(jnp.float32))
        gains += split(gained)
        sums[l] = sums[l] + fold(gained)
        shifts[l] = shifts[l] + fold(weight * shift[l : l + 1, :].astype(jnp.float32))
    ones = jnp.ones((16, rows.shape[1]), jnp.bfloat16)
    reads[...] += dot_lanes(jnp.concatenate(gains + [ones], axis=0), rows)
    gram[...] += dot_lanes(rows, rows)
    column[...] += dot_lanes(rows, jnp.ones((128, rows.shape[1]), jnp.bfloat16))

    @pl.when(step == pl.num_programs(0) - 1)
    def _():
        average = reads[256:257] * (1.0 / width)
        centred = gram[...] * (1.0 / width) - (column[:, :1] * (1.0 / width)) * average
        mixer[:256], mixer[256:512] = split(centred[:256, :256])
        for l in range(lights):
            total = jnp.sum(sums[l], axis=1, keepdims=True)
            read = reads[l * 128 : l * 128 + 64] + reads[l * 128 + 64 : l * 128 + 128]
            read = read - total * average
            start = 512 + l * 128
            mixer[start : start + 64], mixer[start + 64 : start + 128] = split(read[:, :256])
            bias[l] = jnp.broadcast_to(
                jnp.sum(shifts[l], axis=1, keepdims=True), bias.shape[1:]
            )
            tokens = light[l]
            cross[l] = 2.0 * dot_split(centred[:256, 256:], tokens)
            direct[l] = dot_split(read[:, 256:], tokens)
            turned = tokens.astype(jnp.float32).T
            own = jnp.sum(dot_split(centred[256:, 256:], tokens) * turned, axis=0, keepdims=True)
            base[l] = jnp.broadcast_to(own, base.shape[1:])


def render_kernel(ids, a0, a1, a2, a3, mixer, cross, direct, base, bias, attrs, rendered):
    me = ids[0]
    attrs[pl.ds(me, 1)] = a0[...][None]
    attrs[pl.ds(1 - me, 1)] = a1[...][None]
    latents = jnp.concatenate((a0[...], a1[...], a2[...], a3[...]), axis=0)
    mixed = jnp.dot(mixer[...], latents, preferred_element_type=jnp.float32)
    square = mixed[:256] + mixed[256:512]
    wide = latents.astype(jnp.float32)
    for l in range(rendered.shape[0]):
        spread = jnp.sum(wide * (square + cross[l]), axis=0, keepdims=True) + base[l, :1]
        invert = lax.rsqrt(jnp.maximum(spread, 0.0) + EPS)
        start = 512 + l * 128
        read = mixed[start : start + 64] + mixed[start + 64 : start + 128] + direct[l]
        shift = jnp.concatenate([bias[l]] * (read.shape[1] // 128), axis=1)
        rendered[l] = (read * invert + shift).astype(jnp.bfloat16)


LIMIT = pltpu.CompilerParams(vmem_limit_bytes=24 << 20)
RESIDENT = pl.BlockSpec(memory_space=pltpu.VMEM)


def resident(*arrays):
    return [pltpu.with_memory_space_constraint(a, pltpu.VMEM) for a in arrays]


def whole(shape):
    return pl.BlockSpec(shape, lambda *_: (0,) * len(shape))


def on_device(
    q_inv,
    k_inv,
    v_inv,
    group_ids,
    w_attr,
    env_ids,
    env_table,
    w_embed_attr,
    w_embed_env,
    mod_scale,
    mod_shift,
    w_final,
):
    groups, rows, width = q_inv.shape
    heads = width // HD
    first = 3 * rows // 4
    patch = w_attr.shape[2]
    lights, model = mod_scale.shape
    channels = w_embed_env.shape[0]
    me = lax.axis_index("seq") % 2
    grp = lax.axis_index("grp")

    def pick(array, group, start=0, count=rows):
        return lax.dynamic_slice(array, (group, start, 0), (1, count, width))[0]

    same0 = seq_swap(pick(q_inv, me, 0, first), 2)
    cross0 = seq_swap(pick(q_inv, 1 - me, 0, first), 3)
    kx = seq_swap(pick(k_inv, 1 - me), 1)
    vx = seq_swap(pick(v_inv, 1 - me), 1)
    qx = seq_swap(pick(q_inv, 1 - me), 1)

    mine = 2 * grp + me
    others = (mine, 2 * grp + 1 - me, 2 * (1 - grp) + me, 2 * (1 - grp) + 1 - me)
    ids = jnp.stack([me] + [group_ids[n] for n in others]).astype(jnp.int32)

    cols = STEP_HEADS * HD
    steps = heads // STEP_HEADS
    picked = pl.BlockSpec((None, rows, cols), lambda g, s: (s[0], 0, g))
    plain = pl.BlockSpec((rows, cols), lambda g, s: (0, g))
    reads = pl.BlockSpec((STEP_HEADS, 80, 2 * rows), lambda g, s: (g, 0, 0))
    vw, mean, level = pl.pallas_call(
        local_kernel,
        grid_spec=pltpu.PrefetchScalarGridSpec(
            num_scalar_prefetch=1,
            grid=(steps,),
            in_specs=[
                picked,
                plain,
                picked,
                plain,
                picked,
                plain,
                pl.BlockSpec((None, patch, cols), lambda g, s: (s[1], 0, g)),
            ],
            out_specs=[
                reads,
                pl.BlockSpec((STEP_HEADS, 64, 2 * rows), lambda g, s: (g, 0, 0)),
                whole((heads, 2 * rows)),
            ],
        ),
        out_shape=[
            jax.ShapeDtypeStruct((heads, 80, 2 * rows), jnp.bfloat16),
            jax.ShapeDtypeStruct((heads, 64, 2 * rows), jnp.float32),
            jax.ShapeDtypeStruct((heads, 2 * rows), jnp.float32),
        ],
        compiler_params=LIMIT,
        name="local",
    )(ids, q_inv, qx, k_inv, kx, v_inv, vx, jnp.swapaxes(w_attr, 1, 2))

    late_same = pick(q_inv, me, first, rows - first)
    late_cross = pick(q_inv, 1 - me, first, rows - first)
    level, late_same, late_cross = lax.optimization_barrier((level, late_same, late_cross))
    home = seq_swap(level, 2)
    same1 = seq_swap(late_same, 2)
    cross1 = seq_swap(late_cross, 3)

    lighting = jnp.take(env_table, env_ids, axis=0)
    strips = model // CHUNK
    weights = [
        pl.BlockSpec((None, patch, CHUNK), lambda g, s, n=n: (s[1 + n], 0, g))
        for n in range(4)
    ]
    strip = lambda count: pl.BlockSpec((count, CHUNK), lambda g, s: (0, g))
    kinds = 4 * patch
    inputs = kinds + channels
    out_shapes = [
        pltpu.VMEM((2 * kinds + 2 * lights * patch, kinds), jnp.bfloat16),
        pltpu.VMEM((lights, kinds, rows), jnp.float32),
        pltpu.VMEM((lights, patch, rows), jnp.float32),
        pltpu.VMEM((lights, 8, rows), jnp.float32),
        pltpu.VMEM((lights, patch, 128), jnp.float32),
    ]
    prepared = pl.pallas_call(
        prepare_kernel,
        grid_spec=pltpu.PrefetchScalarGridSpec(
            num_scalar_prefetch=1,
            grid=(strips,),
            in_specs=weights
            + [
                strip(channels),
                strip(patch),
                strip(lights),
                strip(lights),
                whole((lights, rows, channels)),
            ],
            out_specs=[whole(s.shape) for s in out_shapes],
            scratch_shapes=[
                pltpu.VMEM((2 * lights * patch + 16, inputs), jnp.float32),
                pltpu.VMEM((inputs, inputs), jnp.float32),
                pltpu.VMEM((inputs, 128), jnp.float32),
                pltpu.VMEM((lights, patch, 128), jnp.float32),
                pltpu.VMEM((lights, patch, 128), jnp.float32),
            ],
        ),
        out_shape=out_shapes,
        compiler_params=LIMIT,
        name="prepare",
    )(
        ids,
        w_embed_attr,
        w_embed_attr,
        w_embed_attr,
        w_embed_attr,
        w_embed_env,
        w_final.T,
        mod_scale,
        mod_shift,
        lighting,
    )

    def remote(same, crossed, spans, lane):
        count = same.shape[0]
        wide = 2 * count
        block = pl.BlockSpec((count, cols), lambda g, s: (0, g))
        sent = pl.pallas_call(
            lambda *refs: remote_kernel(spans, *refs),
            grid_spec=pltpu.PrefetchScalarGridSpec(
                num_scalar_prefetch=1,
                grid=(steps,),
                in_specs=[
                    block,
                    block,
                    picked,
                    plain,
                    reads,
                    pl.BlockSpec((heads, wide), lambda g, s: (0, lane)),
                ],
                out_specs=whole((64 + heads, wide)),
                scratch_shapes=[
                    pltpu.VMEM((64, wide), jnp.float32),
                    pltpu.VMEM((heads, wide), jnp.float32),
                ],
            ),
            out_shape=jax.ShapeDtypeStruct((64 + heads, wide), jnp.bfloat16),
            compiler_params=LIMIT,
            name="remote",
        )(ids, same, crossed, k_inv, kx, vw, home)
        return seq_swap(sent, 2)

    back0 = remote(same0, cross0, ((0, 128), (128, 192)), 0)
    back1 = remote(same1, cross1, ((0, 64),), 3)
    early = pl.pallas_call(
        early_kernel,
        in_specs=[RESIDENT] * 2,
        out_specs=RESIDENT,
        out_shape=pltpu.VMEM((64, 2 * first), jnp.float32),
        compiler_params=LIMIT,
        name="early",
    )(*resident(back0, mean))
    own, other = pl.pallas_call(
        merge_kernel,
        in_specs=[RESIDENT] * 3,
        out_specs=[RESIDENT] * 2,
        out_shape=[pltpu.VMEM((64, rows), jnp.bfloat16)] * 2,
        compiler_params=LIMIT,
        name="merge",
    )(*resident(back1, mean, early))
    a1 = seq_swap(other, 1)
    a2 = grp_swap(own)
    a3 = both_swap(other)
    attrs, rendered = pl.pallas_call(
        render_kernel,
        in_specs=[pl.BlockSpec(memory_space=pltpu.SMEM)] + [RESIDENT] * 9,
        out_specs=[RESIDENT] * 2,
        out_shape=[
            jax.ShapeDtypeStruct((groups, patch, rows), jnp.bfloat16),
            jax.ShapeDtypeStruct((lights, patch, rows), jnp.bfloat16),
        ],
        compiler_params=LIMIT,
        name="render",
    )(ids, *resident(own, a1, a2, a3, *prepared))
    return (jnp.swapaxes(attrs, 1, 2), jnp.swapaxes(rendered, 1, 2))


def solution(mesh):
    in_specs = (
        P("grp", "seq", None),
        P("grp", "seq", None),
        P("grp", "seq", None),
        P(),
        P(),
        P("grp", "seq"),
        P(),
        P(),
        P(),
        P("grp", None),
        P("grp", None),
        P(),
    )
    out_specs = (P("grp", "seq", None), P("grp", "seq", None))
    return jax.shard_map(
        on_device, mesh=mesh, in_specs=in_specs, out_specs=out_specs, check_vma=False
    )
```

```python
import math

import jax
import jax.numpy as jnp
from jax import lax
from jax.experimental import pallas as pl
from jax.experimental.pallas import tpu as pltpu
from jax.sharding import PartitionSpec as P


HD = 128
STEP_HEADS = 4
EPS = 1e-06
SCALE = HD ** (-0.5) * math.log2(math.e)
SAFE = 60.0
CHUNK = 1024
OVER_LANES = (((1,), (1,)), ((), ()))


def seq_swap(block, flip):
    count = lax.axis_size("seq")
    return lax.ppermute(block, "seq", [(i, i ^ flip) for i in range(count)])


def grp_swap(block):
    return lax.ppermute(block, "grp", [(0, 1), (1, 0)])


def both_swap(block):
    count = lax.axis_size("seq")
    route = [
        (g * count + i, (1 - g) * count + (i ^ 1)) for g in range(2) for i in range(count)
    ]
    return lax.ppermute(block, ("grp", "seq"), route)


def dot_lanes(left, right):
    return lax.dot_general(left, right, OVER_LANES, preferred_element_type=jnp.float32)


def split(block):
    high = block.astype(jnp.bfloat16)
    return high, (block - high.astype(jnp.float32)).astype(jnp.bfloat16)


def dot_split(left, right):
    high, low = split(left)
    return dot_lanes(high, right) + dot_lanes(low, right)


def scores_of(keys, queries):
    half = keys.shape[0] // 2
    return [dot_lanes(keys[:half], queries), dot_lanes(keys[half:], queries)]


def plain_softmax(units):
    found = []
    ahead = scores_of(*units[0][:2])
    for n, (_, _, values) in enumerate(units):
        scores = ahead
        if n + 1 < len(units):
            ahead = scores_of(*units[n + 1][:2])
        half = values.shape[1] // 2
        powers = [jnp.exp2(s * SCALE).astype(jnp.bfloat16) for s in scores]
        summed = jnp.dot(
            values[:, :half], powers[0], preferred_element_type=jnp.float32
        ) + jnp.dot(values[:, half:], powers[1], preferred_element_type=jnp.float32)
        total = summed[64:65]
        found.append((summed[:64], total, jnp.log2(total)))
    return found


def shifted_softmax(units):
    found = []
    for keys, queries, values in units:
        scores = dot_lanes(keys, queries)
        top = jnp.max(scores, axis=0, keepdims=True)
        powers = jnp.exp2((scores - top) * SCALE).astype(jnp.bfloat16)
        summed = jnp.dot(values, powers, preferred_element_type=jnp.float32)
        total = summed[64:65]
        found.append((summed[:64], total, top * SCALE + jnp.log2(total)))
    return found


def worst(levels):
    largest = jnp.abs(levels[0])
    for level in levels[1:]:
        largest = jnp.maximum(largest, jnp.abs(level))
    return jnp.max(largest)


def first_kernel(place, q, same, cross, sems):
    me = place[0]
    count = same.shape[0]
    copies = [
        pltpu.make_async_copy(q.at[me, pl.ds(0, count)], same, sems.at[0]),
        pltpu.make_async_copy(q.at[1 - me, pl.ds(0, count)], cross, sems.at[1]),
    ]
    for copy in copies:
        copy.start()
    for copy in copies:
        copy.wait()


def second_kernel(place, q, k, v, same, cross, bundle, sems):
    me = place[0]
    count = same.shape[0]
    rest = pl.ds(q.shape[1] - count, count)
    copies = [
        pltpu.make_async_copy(a.at[1 - me], bundle.at[n], sems.at[n])
        for n, a in enumerate((q, k, v))
    ]
    copies += [
        pltpu.make_async_copy(q.at[me, rest], same, sems.at[3]),
        pltpu.make_async_copy(q.at[1 - me, rest], cross, sems.at[4]),
    ]
    for copy in copies:
        copy.start()
    for copy in copies:
        copy.wait()


def local_kernel(me, grp, kinds, q, qx, k, kx, v, vx, w, vw, mean, level):
    step = pl.program_id(0)
    reads = []

    for i in range(STEP_HEADS):
        cols = slice(i * HD, (i + 1) * HD)
        values = jnp.concatenate((v[:, cols], vx[:, cols]), axis=0)
        read = dot_lanes(w[:, cols], values).astype(jnp.bfloat16)
        read = jnp.concatenate((read, jnp.ones((16, read.shape[1]), jnp.bfloat16)), axis=0)
        vw[i] = read
        reads.append(read)

    def attend(softmax):
        units = []
        for i in range(STEP_HEADS):
            cols = slice(i * HD, (i + 1) * HD)
            keys = jnp.concatenate((k[:, cols], kx[:, cols]), axis=0)
            for spans in (((0, 128),), ((128, 192), (192, 256))):
                pieces = []
                for a, b in spans:
                    pieces += [q[a:b, cols], qx[a:b, cols]]
                units.append((keys, jnp.concatenate(pieces, axis=0), reads[i]))
        found = softmax(units)
        levels = []
        for i in range(STEP_HEADS):
            rows = []
            for n in range(2):
                summed, total, row = found[2 * i + n]
                mean[i, :, n * 256 : n * 256 + 256] = summed * (1.0 / total)
                rows.append(row)
            levels.append(jnp.concatenate(rows, axis=1))
            level[pl.ds(step * STEP_HEADS + i, 1), :] = levels[-1]
        return worst(levels)

    reach = attend(plain_softmax)

    @pl.when(jnp.logical_not(reach < SAFE))
    def _():
        attend(shifted_softmax)


def remote_kernel(spans, me, qs, qd, k, kx, vw, home, out, acc, share):
    step = pl.program_id(0)

    @pl.when(step == 0)
    def _():
        acc[...] = jnp.zeros_like(acc)

    before = acc[...]

    def attend(softmax):
        gathered = [before[:, a * 2 : b * 2] for a, b in spans]
        units = []
        for i in range(STEP_HEADS):
            cols = slice(i * HD, (i + 1) * HD)
            keys = jnp.concatenate((k[:, cols], kx[:, cols]), axis=0)
            for a, b in spans:
                queries = jnp.concatenate((qs[a:b, cols], qd[a:b, cols]), axis=0)
                units.append((keys, queries, vw[i]))
        found = softmax(units)
        levels = []
        for i in range(STEP_HEADS):
            row = pl.ds(step * STEP_HEADS + i, 1)
            theirs = home[row, :]
            rows, mines = [], []
            for n, (a, b) in enumerate(spans):
                summed, total, level = found[i * len(spans) + n]
                mine = 1.0 / (1.0 + jnp.exp2(theirs[:, 2 * a : 2 * b] - level))
                mine = mine.astype(jnp.bfloat16).astype(jnp.float32)
                gathered[n] = gathered[n] + summed * (mine / total)
                mines.append(mine)
                rows.append(level)
            share[row, :] = jnp.concatenate(mines, axis=1)
            levels.append(jnp.concatenate(rows, axis=1))
        for n, (a, b) in enumerate(spans):
            acc[:, 2 * a : 2 * b] = gathered[n]
        return worst(levels)

    reach = attend(plain_softmax)

    @pl.when(jnp.logical_not(reach < SAFE))
    def _():
        attend(shifted_softmax)

    @pl.when(step == pl.num_programs(0) - 1)
    def _():
        out[:64] = acc[...].astype(jnp.bfloat16)
        out[64:] = share[...].astype(jnp.bfloat16)


def blend(remote, mean, start):
    acc = remote[:64].astype(jnp.float32)
    for h in range(mean.shape[0]):
        keep = 1.0 - remote[64 + h : 65 + h].astype(jnp.float32)
        acc = acc + mean[h, :, start : start + acc.shape[1]] * keep
    return acc


def early_kernel(remote, mean, out):
    out[...] = blend(remote, mean, 0)


def merge_kernel(remote, mean, early, own, other):
    late = blend(remote, mean, early.shape[1])
    mixed = early[:, 256:]
    first = lax.broadcasted_iota(jnp.int32, late.shape, 1) < 64
    own[:, :128] = early[:, :128].astype(jnp.bfloat16)
    other[:, :128] = early[:, 128:256].astype(jnp.bfloat16)
    own[:, 128:] = jnp.where(first, mixed, pltpu.roll(late, 64, 1)).astype(jnp.bfloat16)
    other[:, 128:] = jnp.where(first, pltpu.roll(mixed, 64, 1), late).astype(jnp.bfloat16)


def prepare_kernel(
    me, grp, kinds, w0, w1, w2, w3, w_env, final, scale, shift, light,
    mixer, cross, direct, base, bias, reads, gram, column, sums, shifts,
):
    step = pl.program_id(0)
    lights = scale.shape[0]
    width = pl.num_programs(0) * w0.shape[1]

    @pl.when(step == 0)
    def _():
        for ref in (reads, gram, column, sums, shifts):
            ref[...] = jnp.zeros_like(ref)

    rows = jnp.concatenate((w0[...], w1[...], w2[...], w3[...], w_env[...]), axis=0)
    weight = final[...].astype(jnp.float32)

    def fold(block):
        total = block[:, :128]
        for s in range(1, block.shape[1] // 128):
            total = total + block[:, s * 128 : (s + 1) * 128]
        return total

    gains = []
    for l in range(lights):
        gained = weight * (1.0 + scale[l : l + 1, :].astype(jnp.float32))
        gains += split(gained)
        sums[l] = sums[l] + fold(gained)
        shifts[l] = shifts[l] + fold(weight * shift[l : l + 1, :].astype(jnp.float32))
    ones = jnp.ones((16, rows.shape[1]), jnp.bfloat16)
    reads[...] += dot_lanes(jnp.concatenate(gains + [ones], axis=0), rows)
    gram[...] += dot_lanes(rows, rows)
    column[...] += dot_lanes(rows, jnp.ones((128, rows.shape[1]), jnp.bfloat16))

    @pl.when(step == pl.num_programs(0) - 1)
    def _():
        average = reads[256:257] * (1.0 / width)
        centred = gram[...] * (1.0 / width) - (column[:, :1] * (1.0 / width)) * average
        mixer[:256], mixer[256:512] = split(centred[:256, :256])
        for l in range(lights):
            total = jnp.sum(sums[l], axis=1, keepdims=True)
            read = reads[l * 128 : l * 128 + 64] + reads[l * 128 + 64 : l * 128 + 128]
            read = read - total * average
            start = 512 + l * 128
            mixer[start : start + 64], mixer[start + 64 : start + 128] = split(read[:, :256])
            bias[l] = jnp.broadcast_to(
                jnp.sum(shifts[l], axis=1, keepdims=True), bias.shape[1:]
            )
            tokens = light[l]
            cross[l] = 2.0 * dot_split(centred[:256, 256:], tokens)
            direct[l] = dot_split(read[:, 256:], tokens)
            turned = tokens.astype(jnp.float32).T
            own = jnp.sum(dot_split(centred[256:, 256:], tokens) * turned, axis=0, keepdims=True)
            base[l] = jnp.broadcast_to(own, base.shape[1:])


def render_kernel(place, a0, a1, a2, a3, mixer, cross, direct, base, bias, attrs, rendered):
    me = place[0]
    attrs[pl.ds(me, 1)] = a0[...][None]
    attrs[pl.ds(1 - me, 1)] = a1[...][None]
    latents = jnp.concatenate((a0[...], a1[...], a2[...], a3[...]), axis=0)
    mixed = jnp.dot(mixer[...], latents, preferred_element_type=jnp.float32)
    square = mixed[:256] + mixed[256:512]
    wide = latents.astype(jnp.float32)
    for l in range(rendered.shape[0]):
        spread = jnp.sum(wide * (square + cross[l]), axis=0, keepdims=True) + base[l, :1]
        invert = lax.rsqrt(jnp.maximum(spread, 0.0) + EPS)
        start = 512 + l * 128
        read = mixed[start : start + 64] + mixed[start + 64 : start + 128] + direct[l]
        shift = jnp.concatenate([bias[l]] * (read.shape[1] // 128), axis=1)
        rendered[l] = (read * invert + shift).astype(jnp.bfloat16)


LIMIT = pltpu.CompilerParams(vmem_limit_bytes=24 << 20)
RESIDENT = pl.BlockSpec(memory_space=pltpu.VMEM)


def resident(*arrays):
    return [pltpu.with_memory_space_constraint(a, pltpu.VMEM) for a in arrays]


def stay(array):
    return pltpu.with_memory_space_constraint(array, pltpu.HBM)


def whole(shape):
    return pl.BlockSpec(shape, lambda *_: (0,) * len(shape))


def on_device(
    q_inv,
    k_inv,
    v_inv,
    group_ids,
    w_attr,
    env_ids,
    env_table,
    w_embed_attr,
    w_embed_env,
    mod_scale,
    mod_shift,
    w_final,
):
    groups, rows, width = q_inv.shape
    heads = width // HD
    first = 3 * rows // 4
    patch = w_attr.shape[2]
    lights, model = mod_scale.shape
    channels = w_embed_env.shape[0]
    me = lax.axis_index("seq") % 2
    grp = lax.axis_index("grp")

    place = me.reshape(1).astype(jnp.int32)
    side = grp.reshape(1).astype(jnp.int32)
    scalar = pl.BlockSpec(memory_space=pltpu.SMEM)
    remain = pl.BlockSpec(memory_space=pltpu.HBM)
    ahead, behind = pl.pallas_call(
        first_kernel,
        in_specs=[scalar, remain],
        out_specs=[remain] * 2,
        out_shape=[pltpu.HBM((first, width), jnp.bfloat16)] * 2,
        scratch_shapes=[pltpu.SemaphoreType.DMA((2,))],
        compiler_params=LIMIT,
        name="first",
    )(place, stay(q_inv))
    same0 = seq_swap(ahead, 2)
    cross0 = seq_swap(behind, 3)
    late_same, late_cross, bundle = pl.pallas_call(
        second_kernel,
        in_specs=[scalar, remain, remain, remain],
        out_specs=[remain] * 3,
        out_shape=[
            pltpu.HBM((rows - first, width), jnp.bfloat16),
            pltpu.HBM((rows - first, width), jnp.bfloat16),
            pltpu.HBM((3, rows, width), jnp.bfloat16),
        ],
        scratch_shapes=[pltpu.SemaphoreType.DMA((5,))],
        compiler_params=LIMIT,
        name="second",
    )(place, stay(q_inv), stay(k_inv), stay(v_inv))
    bundle = seq_swap(bundle, 1)

    cols = STEP_HEADS * HD
    steps = heads // STEP_HEADS
    picked = pl.BlockSpec((None, rows, cols), lambda g, m, *_: (m[0], 0, g))
    given = [
        pl.BlockSpec((None, rows, cols), lambda g, *_, n=n: (n, 0, g)) for n in range(3)
    ]
    reads = pl.BlockSpec((STEP_HEADS, 80, 2 * rows), lambda g, *_: (g, 0, 0))
    vw, mean, level = pl.pallas_call(
        local_kernel,
        grid_spec=pltpu.PrefetchScalarGridSpec(
            num_scalar_prefetch=3,
            grid=(steps,),
            in_specs=[
                picked,
                given[0],
                picked,
                given[1],
                picked,
                given[2],
                pl.BlockSpec((None, patch, cols), lambda g, m, r, t: (t[2 * r[0] + m[0]], 0, g)),
            ],
            out_specs=[
                reads,
                pl.BlockSpec((STEP_HEADS, 64, 2 * rows), lambda g, *_: (g, 0, 0)),
                whole((heads, 2 * rows)),
            ],
        ),
        out_shape=[
            jax.ShapeDtypeStruct((heads, 80, 2 * rows), jnp.bfloat16),
            jax.ShapeDtypeStruct((heads, 64, 2 * rows), jnp.float32),
            jax.ShapeDtypeStruct((heads, 2 * rows), jnp.float32),
        ],
        compiler_params=LIMIT,
        name="local",
    )(
        place,
        side,
        group_ids,
        stay(q_inv),
        bundle,
        stay(k_inv),
        bundle,
        stay(v_inv),
        bundle,
        stay(jnp.swapaxes(w_attr, 1, 2)),
    )

    level, late_same, late_cross = lax.optimization_barrier((level, late_same, late_cross))
    home = seq_swap(level, 2)
    same1 = seq_swap(late_same, 2)
    cross1 = seq_swap(late_cross, 3)

    lighting = jnp.take(env_table, env_ids, axis=0)
    strips = model // CHUNK
    weights = [
        pl.BlockSpec(
            (None, patch, CHUNK),
            lambda g, m, r, t, n=n: (
                t[2 * (r[0] if n < 2 else 1 - r[0]) + (1 - m[0] if n % 2 else m[0])],
                0,
                g,
            ),
        )
        for n in range(4)
    ]
    strip = lambda count: pl.BlockSpec((count, CHUNK), lambda g, *_: (0, g))
    kinds = 4 * patch
    inputs = kinds + channels
    out_shapes = [
        pltpu.VMEM((2 * kinds + 2 * lights * patch, kinds), jnp.bfloat16),
        pltpu.VMEM((lights, kinds, rows), jnp.float32),
        pltpu.VMEM((lights, patch, rows), jnp.float32),
        pltpu.VMEM((lights, 8, rows), jnp.float32),
        pltpu.VMEM((lights, patch, 128), jnp.float32),
    ]
    prepared = pl.pallas_call(
        prepare_kernel,
        grid_spec=pltpu.PrefetchScalarGridSpec(
            num_scalar_prefetch=3,
            grid=(strips,),
            in_specs=weights
            + [
                strip(channels),
                strip(patch),
                strip(lights),
                strip(lights),
                whole((lights, rows, channels)),
            ],
            out_specs=[whole(s.shape) for s in out_shapes],
            scratch_shapes=[
                pltpu.VMEM((2 * lights * patch + 16, inputs), jnp.float32),
                pltpu.VMEM((inputs, inputs), jnp.float32),
                pltpu.VMEM((inputs, 128), jnp.float32),
                pltpu.VMEM((lights, patch, 128), jnp.float32),
                pltpu.VMEM((lights, patch, 128), jnp.float32),
            ],
        ),
        out_shape=out_shapes,
        compiler_params=LIMIT,
        name="prepare",
    )(
        place,
        side,
        group_ids,
        w_embed_attr,
        w_embed_attr,
        w_embed_attr,
        w_embed_attr,
        w_embed_env,
        w_final.T,
        mod_scale,
        mod_shift,
        lighting,
    )

    def remote(same, crossed, spans, lane):
        count = same.shape[0]
        wide = 2 * count
        block = pl.BlockSpec((count, cols), lambda g, m: (0, g))
        sent = pl.pallas_call(
            lambda *refs: remote_kernel(spans, *refs),
            grid_spec=pltpu.PrefetchScalarGridSpec(
                num_scalar_prefetch=1,
                grid=(steps,),
                in_specs=[
                    block,
                    block,
                    picked,
                    given[1],
                    reads,
                    pl.BlockSpec((heads, wide), lambda g, m: (0, lane)),
                ],
                out_specs=whole((64 + heads, wide)),
                scratch_shapes=[
                    pltpu.VMEM((64, wide), jnp.float32),
                    pltpu.VMEM((heads, wide), jnp.float32),
                ],
            ),
            out_shape=jax.ShapeDtypeStruct((64 + heads, wide), jnp.bfloat16),
            compiler_params=LIMIT,
            name="remote",
        )(place, same, crossed, k_inv, bundle, vw, home)
        return seq_swap(sent, 2)

    back0 = remote(same0, cross0, ((0, 128), (128, 192)), 0)
    back1 = remote(same1, cross1, ((0, 64),), 3)
    early = pl.pallas_call(
        early_kernel,
        in_specs=[RESIDENT] * 2,
        out_specs=RESIDENT,
        out_shape=pltpu.VMEM((64, 2 * first), jnp.float32),
        compiler_params=LIMIT,
        name="early",
    )(*resident(back0, mean))
    own, other = pl.pallas_call(
        merge_kernel,
        in_specs=[RESIDENT] * 3,
        out_specs=[RESIDENT] * 2,
        out_shape=[pltpu.VMEM((64, rows), jnp.bfloat16)] * 2,
        compiler_params=LIMIT,
        name="merge",
    )(*resident(back1, mean, early))
    a1 = seq_swap(other, 1)
    a2 = grp_swap(own)
    a3 = both_swap(other)
    attrs, rendered = pl.pallas_call(
        render_kernel,
        in_specs=[pl.BlockSpec(memory_space=pltpu.SMEM)] + [RESIDENT] * 9,
        out_specs=[RESIDENT] * 2,
        out_shape=[
            jax.ShapeDtypeStruct((groups, patch, rows), jnp.bfloat16),
            jax.ShapeDtypeStruct((lights, patch, rows), jnp.bfloat16),
        ],
        compiler_params=LIMIT,
        name="render",
    )(place, *resident(own, a1, a2, a3, *prepared))
    return (jnp.swapaxes(attrs, 1, 2), jnp.swapaxes(rendered, 1, 2))


def solution(mesh):
    in_specs = (
        P("grp", "seq", None),
        P("grp", "seq", None),
        P("grp", "seq", None),
        P(),
        P(),
        P("grp", "seq"),
        P(),
        P(),
        P(),
        P("grp", None),
        P("grp", None),
        P(),
    )
    out_specs = (P("grp", "seq", None), P("grp", "seq", None))
    return jax.shard_map(
        on_device, mesh=mesh, in_specs=in_specs, out_specs=out_specs, check_vma=False
    )
```

```python
import math

import jax
import jax.numpy as jnp
from jax import lax
from jax.experimental import pallas as pl
from jax.experimental.pallas import tpu as pltpu
from jax.sharding import PartitionSpec as P


HD = 128
STEP_HEADS = 4
EPS = 1e-06
SCALE = HD ** (-0.5) * math.log2(math.e)
SAFE = 60.0
CHUNK = 1024
OVER_LANES = (((1,), (1,)), ((), ()))


def seq_swap(block, flip):
    count = lax.axis_size("seq")
    return lax.ppermute(block, "seq", [(i, i ^ flip) for i in range(count)])


def grp_swap(block):
    return lax.ppermute(block, "grp", [(0, 1), (1, 0)])


def both_swap(block):
    count = lax.axis_size("seq")
    route = [
        (g * count + i, (1 - g) * count + (i ^ 1)) for g in range(2) for i in range(count)
    ]
    return lax.ppermute(block, ("grp", "seq"), route)


def dot_lanes(left, right):
    return lax.dot_general(left, right, OVER_LANES, preferred_element_type=jnp.float32)


def split(block):
    high = block.astype(jnp.bfloat16)
    return high, (block - high.astype(jnp.float32)).astype(jnp.bfloat16)


def dot_split(left, right):
    high, low = split(left)
    return dot_lanes(high, right) + dot_lanes(low, right)


def scores_of(keys, queries):
    half = keys.shape[0] // 2
    return [dot_lanes(keys[:half], queries), dot_lanes(keys[half:], queries)]


def plain_softmax(units):
    found = []
    ahead = scores_of(*units[0][:2])
    for n, (_, _, values) in enumerate(units):
        scores = ahead
        if n + 1 < len(units):
            ahead = scores_of(*units[n + 1][:2])
        half = values.shape[1] // 2
        powers = [jnp.exp2(s * SCALE).astype(jnp.bfloat16) for s in scores]
        summed = jnp.dot(
            values[:, :half], powers[0], preferred_element_type=jnp.float32
        ) + jnp.dot(values[:, half:], powers[1], preferred_element_type=jnp.float32)
        total = summed[64:65]
        found.append((summed[:64], total, jnp.log2(total)))
    return found


def shifted_softmax(units):
    found = []
    for keys, queries, values in units:
        scores = dot_lanes(keys, queries)
        top = jnp.max(scores, axis=0, keepdims=True)
        powers = jnp.exp2((scores - top) * SCALE).astype(jnp.bfloat16)
        summed = jnp.dot(values, powers, preferred_element_type=jnp.float32)
        total = summed[64:65]
        found.append((summed[:64], total, top * SCALE + jnp.log2(total)))
    return found


def worst(levels):
    largest = jnp.abs(levels[0])
    for level in levels[1:]:
        largest = jnp.maximum(largest, jnp.abs(level))
    return jnp.max(largest)


def shuttle(pieces, arrive, leave):
    inward = [
        pltpu.make_async_copy(source, held, arrive.at[n])
        for n, (source, held, _) in enumerate(pieces)
    ]
    outward = [
        pltpu.make_async_copy(held, target, leave.at[n])
        for n, (_, held, target) in enumerate(pieces)
    ]
    for copy in inward:
        copy.start()
    for here, there in zip(inward, outward):
        here.wait()
        there.start()
    for copy in outward:
        copy.wait()


def first_kernel(place, q, same, cross, held, arrive, leave):
    me = place[0]
    count = same.shape[0] // 2
    pieces = []
    for n, (group, target) in enumerate(((me, same), (1 - me, cross))):
        for half in range(2):
            span = pl.ds(half * count, count)
            pieces.append((q.at[group, span], held.at[n, span], target.at[span]))
    shuttle(pieces, arrive, leave)


def second_kernel(place, q, k, v, same, cross, bundle, held, rest, arrive, leave):
    me = place[0]
    count = same.shape[0]
    tail = pl.ds(q.shape[1] - count, count)
    pieces = [(a.at[1 - me], held.at[n], bundle.at[n]) for n, a in enumerate((q, k, v))]
    pieces.append((q.at[me, tail], rest.at[0], same))
    pieces.append((q.at[1 - me, tail], rest.at[1], cross))
    shuttle(pieces, arrive, leave)


def local_kernel(me, grp, kinds, q, qx, k, kx, v, vx, w, vw, mean, level):
    step = pl.program_id(0)
    reads = []

    for i in range(STEP_HEADS):
        cols = slice(i * HD, (i + 1) * HD)
        values = jnp.concatenate((v[:, cols], vx[:, cols]), axis=0)
        read = dot_lanes(w[:, cols], values).astype(jnp.bfloat16)
        read = jnp.concatenate((read, jnp.ones((16, read.shape[1]), jnp.bfloat16)), axis=0)
        vw[i] = read
        reads.append(read)

    def attend(softmax):
        units = []
        for i in range(STEP_HEADS):
            cols = slice(i * HD, (i + 1) * HD)
            keys = jnp.concatenate((k[:, cols], kx[:, cols]), axis=0)
            for spans in (((0, 128),), ((128, 192), (192, 256))):
                pieces = []
                for a, b in spans:
                    pieces += [q[a:b, cols], qx[a:b, cols]]
                units.append((keys, jnp.concatenate(pieces, axis=0), reads[i]))
        found = softmax(units)
        levels = []
        for i in range(STEP_HEADS):
            rows = []
            for n in range(2):
                summed, total, row = found[2 * i + n]
                mean[i, :, n * 256 : n * 256 + 256] = summed * (1.0 / total)
                rows.append(row)
            levels.append(jnp.concatenate(rows, axis=1))
            level[pl.ds(step * STEP_HEADS + i, 1), :] = levels[-1]
        return worst(levels)

    reach = attend(plain_softmax)

    @pl.when(jnp.logical_not(reach < SAFE))
    def _():
        attend(shifted_softmax)


def remote_kernel(spans, me, qs, qd, k, kx, vw, home, out, acc, share):
    step = pl.program_id(0)

    @pl.when(step == 0)
    def _():
        acc[...] = jnp.zeros_like(acc)

    before = acc[...]

    def attend(softmax):
        gathered = [before[:, a * 2 : b * 2] for a, b in spans]
        units = []
        for i in range(STEP_HEADS):
            cols = slice(i * HD, (i + 1) * HD)
            keys = jnp.concatenate((k[:, cols], kx[:, cols]), axis=0)
            for a, b in spans:
                queries = jnp.concatenate((qs[a:b, cols], qd[a:b, cols]), axis=0)
                units.append((keys, queries, vw[i]))
        found = softmax(units)
        levels = []
        for i in range(STEP_HEADS):
            row = pl.ds(step * STEP_HEADS + i, 1)
            theirs = home[row, :]
            rows, mines = [], []
            for n, (a, b) in enumerate(spans):
                summed, total, level = found[i * len(spans) + n]
                mine = 1.0 / (1.0 + jnp.exp2(theirs[:, 2 * a : 2 * b] - level))
                mine = mine.astype(jnp.bfloat16).astype(jnp.float32)
                gathered[n] = gathered[n] + summed * (mine / total)
                mines.append(mine)
                rows.append(level)
            share[row, :] = jnp.concatenate(mines, axis=1)
            levels.append(jnp.concatenate(rows, axis=1))
        for n, (a, b) in enumerate(spans):
            acc[:, 2 * a : 2 * b] = gathered[n]
        return worst(levels)

    reach = attend(plain_softmax)

    @pl.when(jnp.logical_not(reach < SAFE))
    def _():
        attend(shifted_softmax)

    @pl.when(step == pl.num_programs(0) - 1)
    def _():
        out[:64] = acc[...].astype(jnp.bfloat16)
        out[64:] = share[...].astype(jnp.bfloat16)


def blend(remote, mean, start):
    acc = remote[:64].astype(jnp.float32)
    for h in range(mean.shape[0]):
        keep = 1.0 - remote[64 + h : 65 + h].astype(jnp.float32)
        acc = acc + mean[h, :, start : start + acc.shape[1]] * keep
    return acc


def early_kernel(remote, mean, out):
    out[...] = blend(remote, mean, 0)


def merge_kernel(remote, mean, early, own, other):
    late = blend(remote, mean, early.shape[1])
    mixed = early[:, 256:]
    first = lax.broadcasted_iota(jnp.int32, late.shape, 1) < 64
    own[:, :128] = early[:, :128].astype(jnp.bfloat16)
    other[:, :128] = early[:, 128:256].astype(jnp.bfloat16)
    own[:, 128:] = jnp.where(first, mixed, pltpu.roll(late, 64, 1)).astype(jnp.bfloat16)
    other[:, 128:] = jnp.where(first, pltpu.roll(mixed, 64, 1), late).astype(jnp.bfloat16)


def prepare_kernel(
    me, grp, kinds, w0, w1, w2, w3, w_env, final, scale, shift, light,
    mixer, cross, direct, base, bias, reads, gram, column, sums, shifts,
):
    step = pl.program_id(0)
    lights = scale.shape[0]
    width = pl.num_programs(0) * w0.shape[1]

    @pl.when(step == 0)
    def _():
        for ref in (reads, gram, column, sums, shifts):
            ref[...] = jnp.zeros_like(ref)

    rows = jnp.concatenate((w0[...], w1[...], w2[...], w3[...], w_env[...]), axis=0)
    weight = final[...].astype(jnp.float32)

    def fold(block):
        total = block[:, :128]
        for s in range(1, block.shape[1] // 128):
            total = total + block[:, s * 128 : (s + 1) * 128]
        return total

    gains = []
    for l in range(lights):
        gained = weight * (1.0 + scale[l : l + 1, :].astype(jnp.float32))
        gains += split(gained)
        sums[l] = sums[l] + fold(gained)
        shifts[l] = shifts[l] + fold(weight * shift[l : l + 1, :].astype(jnp.float32))
    ones = jnp.ones((16, rows.shape[1]), jnp.bfloat16)
    reads[...] += dot_lanes(jnp.concatenate(gains + [ones], axis=0), rows)
    gram[...] += dot_lanes(rows, rows)
    column[...] += dot_lanes(rows, jnp.ones((128, rows.shape[1]), jnp.bfloat16))

    @pl.when(step == pl.num_programs(0) - 1)
    def _():
        average = reads[256:257] * (1.0 / width)
        centred = gram[...] * (1.0 / width) - (column[:, :1] * (1.0 / width)) * average
        mixer[:256], mixer[256:512] = split(centred[:256, :256])
        for l in range(lights):
            total = jnp.sum(sums[l], axis=1, keepdims=True)
            read = reads[l * 128 : l * 128 + 64] + reads[l * 128 + 64 : l * 128 + 128]
            read = read - total * average
            start = 512 + l * 128
            mixer[start : start + 64], mixer[start + 64 : start + 128] = split(read[:, :256])
            bias[l] = jnp.broadcast_to(
                jnp.sum(shifts[l], axis=1, keepdims=True), bias.shape[1:]
            )
            tokens = light[l]
            cross[l] = 2.0 * dot_split(centred[:256, 256:], tokens)
            direct[l] = dot_split(read[:, 256:], tokens)
            turned = tokens.astype(jnp.float32).T
            own = jnp.sum(dot_split(centred[256:, 256:], tokens) * turned, axis=0, keepdims=True)
            base[l] = jnp.broadcast_to(own, base.shape[1:])


def render_kernel(place, a0, a1, a2, a3, mixer, cross, direct, base, bias, attrs, rendered):
    me = place[0]
    attrs[pl.ds(me, 1)] = a0[...][None]
    attrs[pl.ds(1 - me, 1)] = a1[...][None]
    latents = jnp.concatenate((a0[...], a1[...], a2[...], a3[...]), axis=0)
    mixed = jnp.dot(mixer[...], latents, preferred_element_type=jnp.float32)
    square = mixed[:256] + mixed[256:512]
    wide = latents.astype(jnp.float32)
    for l in range(rendered.shape[0]):
        spread = jnp.sum(wide * (square + cross[l]), axis=0, keepdims=True) + base[l, :1]
        invert = lax.rsqrt(jnp.maximum(spread, 0.0) + EPS)
        start = 512 + l * 128
        read = mixed[start : start + 64] + mixed[start + 64 : start + 128] + direct[l]
        shift = jnp.concatenate([bias[l]] * (read.shape[1] // 128), axis=1)
        rendered[l] = (read * invert + shift).astype(jnp.bfloat16)


LIMIT = pltpu.CompilerParams(vmem_limit_bytes=24 << 20)
RESIDENT = pl.BlockSpec(memory_space=pltpu.VMEM)


def resident(*arrays):
    return [pltpu.with_memory_space_constraint(a, pltpu.VMEM) for a in arrays]


def stay(array):
    return pltpu.with_memory_space_constraint(array, pltpu.HBM)


def whole(shape):
    return pl.BlockSpec(shape, lambda *_: (0,) * len(shape))


def on_device(
    q_inv,
    k_inv,
    v_inv,
    group_ids,
    w_attr,
    env_ids,
    env_table,
    w_embed_attr,
    w_embed_env,
    mod_scale,
    mod_shift,
    w_final,
):
    groups, rows, width = q_inv.shape
    heads = width // HD
    first = 3 * rows // 4
    patch = w_attr.shape[2]
    lights, model = mod_scale.shape
    channels = w_embed_env.shape[0]
    me = lax.axis_index("seq") % 2
    grp = lax.axis_index("grp")

    place = me.reshape(1).astype(jnp.int32)
    side = grp.reshape(1).astype(jnp.int32)
    scalar = pl.BlockSpec(memory_space=pltpu.SMEM)
    remain = pl.BlockSpec(memory_space=pltpu.HBM)
    ahead, behind = pl.pallas_call(
        first_kernel,
        in_specs=[scalar, remain],
        out_specs=[remain] * 2,
        out_shape=[pltpu.HBM((first, width), jnp.bfloat16)] * 2,
        scratch_shapes=[pltpu.VMEM((2, first, width), jnp.bfloat16)]
        + [pltpu.SemaphoreType.DMA((4,))] * 2,
        compiler_params=LIMIT,
        name="first",
    )(place, stay(q_inv))
    same0 = seq_swap(ahead, 2)
    cross0 = seq_swap(behind, 3)
    late_same, late_cross, bundle = pl.pallas_call(
        second_kernel,
        in_specs=[scalar, remain, remain, remain],
        out_specs=[remain] * 3,
        out_shape=[
            pltpu.HBM((rows - first, width), jnp.bfloat16),
            pltpu.HBM((rows - first, width), jnp.bfloat16),
            pltpu.HBM((3, rows, width), jnp.bfloat16),
        ],
        scratch_shapes=[
            pltpu.VMEM((3, rows, width), jnp.bfloat16),
            pltpu.VMEM((2, rows - first, width), jnp.bfloat16),
        ]
        + [pltpu.SemaphoreType.DMA((5,))] * 2,
        compiler_params=LIMIT,
        name="second",
    )(place, stay(q_inv), stay(k_inv), stay(v_inv))
    bundle = seq_swap(bundle, 1)

    cols = STEP_HEADS * HD
    steps = heads // STEP_HEADS
    picked = pl.BlockSpec((None, rows, cols), lambda g, m, *_: (m[0], 0, g))
    given = [
        pl.BlockSpec((None, rows, cols), lambda g, *_, n=n: (n, 0, g)) for n in range(3)
    ]
    reads = pl.BlockSpec((STEP_HEADS, 80, 2 * rows), lambda g, *_: (g, 0, 0))
    vw, mean, level = pl.pallas_call(
        local_kernel,
        grid_spec=pltpu.PrefetchScalarGridSpec(
            num_scalar_prefetch=3,
            grid=(steps,),
            in_specs=[
                picked,
                given[0],
                picked,
                given[1],
                picked,
                given[2],
                pl.BlockSpec((None, patch, cols), lambda g, m, r, t: (t[2 * r[0] + m[0]], 0, g)),
            ],
            out_specs=[
                reads,
                pl.BlockSpec((STEP_HEADS, 64, 2 * rows), lambda g, *_: (g, 0, 0)),
                whole((heads, 2 * rows)),
            ],
        ),
        out_shape=[
            jax.ShapeDtypeStruct((heads, 80, 2 * rows), jnp.bfloat16),
            jax.ShapeDtypeStruct((heads, 64, 2 * rows), jnp.float32),
            jax.ShapeDtypeStruct((heads, 2 * rows), jnp.float32),
        ],
        compiler_params=LIMIT,
        name="local",
    )(
        place,
        side,
        group_ids,
        stay(q_inv),
        bundle,
        stay(k_inv),
        bundle,
        stay(v_inv),
        bundle,
        stay(jnp.swapaxes(w_attr, 1, 2)),
    )

    level, late_same, late_cross = lax.optimization_barrier((level, late_same, late_cross))
    home = seq_swap(level, 2)
    same1 = seq_swap(late_same, 2)
    cross1 = seq_swap(late_cross, 3)

    lighting = jnp.take(env_table, env_ids, axis=0)
    strips = model // CHUNK
    weights = [
        pl.BlockSpec(
            (None, patch, CHUNK),
            lambda g, m, r, t, n=n: (
                t[2 * (r[0] if n < 2 else 1 - r[0]) + (1 - m[0] if n % 2 else m[0])],
                0,
                g,
            ),
        )
        for n in range(4)
    ]
    strip = lambda count: pl.BlockSpec((count, CHUNK), lambda g, *_: (0, g))
    kinds = 4 * patch
    inputs = kinds + channels
    out_shapes = [
        pltpu.VMEM((2 * kinds + 2 * lights * patch, kinds), jnp.bfloat16),
        pltpu.VMEM((lights, kinds, rows), jnp.float32),
        pltpu.VMEM((lights, patch, rows), jnp.float32),
        pltpu.VMEM((lights, 8, rows), jnp.float32),
        pltpu.VMEM((lights, patch, 128), jnp.float32),
    ]
    prepared = pl.pallas_call(
        prepare_kernel,
        grid_spec=pltpu.PrefetchScalarGridSpec(
            num_scalar_prefetch=3,
            grid=(strips,),
            in_specs=weights
            + [
                strip(channels),
                strip(patch),
                strip(lights),
                strip(lights),
                whole((lights, rows, channels)),
            ],
            out_specs=[whole(s.shape) for s in out_shapes],
            scratch_shapes=[
                pltpu.VMEM((2 * lights * patch + 16, inputs), jnp.float32),
                pltpu.VMEM((inputs, inputs), jnp.float32),
                pltpu.VMEM((inputs, 128), jnp.float32),
                pltpu.VMEM((lights, patch, 128), jnp.float32),
                pltpu.VMEM((lights, patch, 128), jnp.float32),
            ],
        ),
        out_shape=out_shapes,
        compiler_params=LIMIT,
        name="prepare",
    )(
        place,
        side,
        group_ids,
        w_embed_attr,
        w_embed_attr,
        w_embed_attr,
        w_embed_attr,
        w_embed_env,
        w_final.T,
        mod_scale,
        mod_shift,
        lighting,
    )

    def remote(same, crossed, spans, lane):
        count = same.shape[0]
        wide = 2 * count
        block = pl.BlockSpec((count, cols), lambda g, m: (0, g))
        sent = pl.pallas_call(
            lambda *refs: remote_kernel(spans, *refs),
            grid_spec=pltpu.PrefetchScalarGridSpec(
                num_scalar_prefetch=1,
                grid=(steps,),
                in_specs=[
                    block,
                    block,
                    picked,
                    given[1],
                    reads,
                    pl.BlockSpec((heads, wide), lambda g, m: (0, lane)),
                ],
                out_specs=whole((64 + heads, wide)),
                scratch_shapes=[
                    pltpu.VMEM((64, wide), jnp.float32),
                    pltpu.VMEM((heads, wide), jnp.float32),
                ],
            ),
            out_shape=jax.ShapeDtypeStruct((64 + heads, wide), jnp.bfloat16),
            compiler_params=LIMIT,
            name="remote",
        )(place, same, crossed, k_inv, bundle, vw, home)
        return seq_swap(sent, 2)

    back0 = remote(same0, cross0, ((0, 128), (128, 192)), 0)
    back1 = remote(same1, cross1, ((0, 64),), 3)
    early = pl.pallas_call(
        early_kernel,
        in_specs=[RESIDENT] * 2,
        out_specs=RESIDENT,
        out_shape=pltpu.VMEM((64, 2 * first), jnp.float32),
        compiler_params=LIMIT,
        name="early",
    )(*resident(back0, mean))
    own, other = pl.pallas_call(
        merge_kernel,
        in_specs=[RESIDENT] * 3,
        out_specs=[RESIDENT] * 2,
        out_shape=[pltpu.VMEM((64, rows), jnp.bfloat16)] * 2,
        compiler_params=LIMIT,
        name="merge",
    )(*resident(back1, mean, early))
    a1 = seq_swap(other, 1)
    a2 = grp_swap(own)
    a3 = both_swap(other)
    attrs, rendered = pl.pallas_call(
        render_kernel,
        in_specs=[pl.BlockSpec(memory_space=pltpu.SMEM)] + [RESIDENT] * 9,
        out_specs=[RESIDENT] * 2,
        out_shape=[
            jax.ShapeDtypeStruct((groups, patch, rows), jnp.bfloat16),
            jax.ShapeDtypeStruct((lights, patch, rows), jnp.bfloat16),
        ],
        compiler_params=LIMIT,
        name="render",
    )(place, *resident(own, a1, a2, a3, *prepared))
    return (jnp.swapaxes(attrs, 1, 2), jnp.swapaxes(rendered, 1, 2))


def solution(mesh):
    in_specs = (
        P("grp", "seq", None),
        P("grp", "seq", None),
        P("grp", "seq", None),
        P(),
        P(),
        P("grp", "seq"),
        P(),
        P(),
        P(),
        P("grp", None),
        P("grp", None),
        P(),
    )
    out_specs = (P("grp", "seq", None), P("grp", "seq", None))
    return jax.shard_map(
        on_device, mesh=mesh, in_specs=in_specs, out_specs=out_specs, check_vma=False
    )
```

```python
import math

import jax
import jax.numpy as jnp
from jax import lax
from jax.experimental import pallas as pl
from jax.experimental.pallas import tpu as pltpu
from jax.sharding import PartitionSpec as P


HD = 128
STEP_HEADS = 4
EPS = 1e-06
SCALE = HD ** (-0.5) * math.log2(math.e)
SAFE = 60.0
CHUNK = 1024
OVER_LANES = (((1,), (1,)), ((), ()))


def seq_swap(block, flip):
    count = lax.axis_size("seq")
    return lax.ppermute(block, "seq", [(i, i ^ flip) for i in range(count)])


def grp_swap(block):
    return lax.ppermute(block, "grp", [(0, 1), (1, 0)])


def both_swap(block):
    count = lax.axis_size("seq")
    route = [
        (g * count + i, (1 - g) * count + (i ^ 1)) for g in range(2) for i in range(count)
    ]
    return lax.ppermute(block, ("grp", "seq"), route)


def dot_lanes(left, right):
    return lax.dot_general(left, right, OVER_LANES, preferred_element_type=jnp.float32)


def split(block):
    high = block.astype(jnp.bfloat16)
    return high, (block - high.astype(jnp.float32)).astype(jnp.bfloat16)


def dot_split(left, right):
    high, low = split(left)
    return dot_lanes(high, right) + dot_lanes(low, right)


def scores_of(keys, queries):
    half = keys.shape[0] // 2
    return [dot_lanes(keys[:half], queries), dot_lanes(keys[half:], queries)]


def plain_softmax(units):
    found = []
    ahead = scores_of(*units[0][:2])
    for n, (_, _, values) in enumerate(units):
        scores = ahead
        if n + 1 < len(units):
            ahead = scores_of(*units[n + 1][:2])
        half = values.shape[1] // 2
        powers = [jnp.exp2(s * SCALE).astype(jnp.bfloat16) for s in scores]
        summed = jnp.dot(
            values[:, :half], powers[0], preferred_element_type=jnp.float32
        ) + jnp.dot(values[:, half:], powers[1], preferred_element_type=jnp.float32)
        total = summed[64:65]
        found.append((summed[:64], total, jnp.log2(total)))
    return found


def shifted_softmax(units):
    found = []
    for keys, queries, values in units:
        scores = dot_lanes(keys, queries)
        top = jnp.max(scores, axis=0, keepdims=True)
        powers = jnp.exp2((scores - top) * SCALE).astype(jnp.bfloat16)
        summed = jnp.dot(values, powers, preferred_element_type=jnp.float32)
        total = summed[64:65]
        found.append((summed[:64], total, top * SCALE + jnp.log2(total)))
    return found


def worst(levels):
    largest = jnp.abs(levels[0])
    for level in levels[1:]:
        largest = jnp.maximum(largest, jnp.abs(level))
    return jnp.max(largest)


def shuttle(pieces, arrive, leave):
    inward = [
        pltpu.make_async_copy(source, held, arrive.at[n])
        for n, (source, held, _) in enumerate(pieces)
    ]
    outward = [
        pltpu.make_async_copy(held, target, leave.at[n])
        for n, (_, held, target) in enumerate(pieces)
    ]
    for copy in inward:
        copy.start()
    for here, there in zip(inward, outward):
        here.wait()
        there.start()
    for copy in outward:
        copy.wait()


def first_kernel(place, q, same, cross, arrive):
    me = place[0]
    rows = pl.ds(0, same.shape[0])
    copies = [
        pltpu.make_async_copy(q.at[me, rows], same, arrive.at[0]),
        pltpu.make_async_copy(q.at[1 - me, rows], cross, arrive.at[1]),
    ]
    for copy in copies:
        copy.start()
    for copy in copies:
        copy.wait()


def second_kernel(place, q, k, v, same, cross, bundle, held, rest, arrive, leave):
    me = place[0]
    count = same.shape[0]
    tail = pl.ds(q.shape[1] - count, count)
    pieces = [(a.at[1 - me], held.at[n], bundle.at[n]) for n, a in enumerate((q, k, v))]
    pieces.append((q.at[me, tail], rest.at[0], same))
    pieces.append((q.at[1 - me, tail], rest.at[1], cross))
    shuttle(pieces, arrive, leave)


def local_kernel(me, grp, kinds, q, qx, k, kx, v, vx, w, vw, mean, level):
    step = pl.program_id(0)
    reads = []

    for i in range(STEP_HEADS):
        cols = slice(i * HD, (i + 1) * HD)
        values = jnp.concatenate((v[:, cols], vx[:, cols]), axis=0)
        read = dot_lanes(w[:, cols], values).astype(jnp.bfloat16)
        read = jnp.concatenate((read, jnp.ones((16, read.shape[1]), jnp.bfloat16)), axis=0)
        vw[i] = read
        reads.append(read)

    def attend(softmax):
        units = []
        for i in range(STEP_HEADS):
            cols = slice(i * HD, (i + 1) * HD)
            keys = jnp.concatenate((k[:, cols], kx[:, cols]), axis=0)
            for spans in (((0, 128),), ((128, 192), (192, 256))):
                pieces = []
                for a, b in spans:
                    pieces += [q[a:b, cols], qx[a:b, cols]]
                units.append((keys, jnp.concatenate(pieces, axis=0), reads[i]))
        found = softmax(units)
        levels = []
        for i in range(STEP_HEADS):
            rows = []
            for n in range(2):
                summed, total, row = found[2 * i + n]
                mean[i, :, n * 256 : n * 256 + 256] = summed * (1.0 / total)
                rows.append(row)
            levels.append(jnp.concatenate(rows, axis=1))
            level[pl.ds(step * STEP_HEADS + i, 1), :] = levels[-1]
        return worst(levels)

    reach = attend(plain_softmax)

    @pl.when(jnp.logical_not(reach < SAFE))
    def _():
        attend(shifted_softmax)


def remote_kernel(spans, me, qs, qd, k, kx, vw, home, out, acc, share):
    step = pl.program_id(0)

    @pl.when(step == 0)
    def _():
        acc[...] = jnp.zeros_like(acc)

    before = acc[...]

    def attend(softmax):
        gathered = [before[:, a * 2 : b * 2] for a, b in spans]
        units = []
        for i in range(STEP_HEADS):
            cols = slice(i * HD, (i + 1) * HD)
            keys = jnp.concatenate((k[:, cols], kx[:, cols]), axis=0)
            for a, b in spans:
                queries = jnp.concatenate((qs[a:b, cols], qd[a:b, cols]), axis=0)
                units.append((keys, queries, vw[i]))
        found = softmax(units)
        levels = []
        for i in range(STEP_HEADS):
            row = pl.ds(step * STEP_HEADS + i, 1)
            theirs = home[row, :]
            rows, mines = [], []
            for n, (a, b) in enumerate(spans):
                summed, total, level = found[i * len(spans) + n]
                mine = 1.0 / (1.0 + jnp.exp2(theirs[:, 2 * a : 2 * b] - level))
                mine = mine.astype(jnp.bfloat16).astype(jnp.float32)
                gathered[n] = gathered[n] + summed * (mine / total)
                mines.append(mine)
                rows.append(level)
            share[row, :] = jnp.concatenate(mines, axis=1)
            levels.append(jnp.concatenate(rows, axis=1))
        for n, (a, b) in enumerate(spans):
            acc[:, 2 * a : 2 * b] = gathered[n]
        return worst(levels)

    reach = attend(plain_softmax)

    @pl.when(jnp.logical_not(reach < SAFE))
    def _():
        attend(shifted_softmax)

    @pl.when(step == pl.num_programs(0) - 1)
    def _():
        out[:64] = acc[...].astype(jnp.bfloat16)
        out[64:] = share[...].astype(jnp.bfloat16)


def last_kernel(place, qs, qd, k, kx, vw, home, out, acc, share):
    me = place[0]
    heads = vw.shape[0]
    zero = jnp.zeros((2 * qs.shape[0], HD), jnp.bfloat16)

    def scores_at(start):
        cols = pl.ds(start, 2 * HD)
        keys = jnp.concatenate((k[me, :, cols], kx[:, cols]), axis=0)
        pair = jnp.concatenate((qs[:, cols], qd[:, cols]), axis=0)
        queries = jnp.concatenate(
            (
                jnp.concatenate((pair[:, :HD], zero), axis=1),
                jnp.concatenate((zero, pair[:, HD:]), axis=1),
            ),
            axis=0,
        )
        half = keys.shape[0] // 2
        return [dot_lanes(keys[:half], queries), dot_lanes(keys[half:], queries)]

    def finish(head, scores, top):
        wide = scores[0].shape[1] // 2
        powers = []
        for block in scores:
            shifted = block if top is None else block - top
            powers.append(jnp.exp2(shifted * SCALE).astype(jnp.bfloat16))
        found = []
        for n in range(2):
            read = vw[head + n]
            half = read.shape[1] // 2
            lanes = slice(n * wide, (n + 1) * wide)
            summed = jnp.dot(
                read[:, :half], powers[0][:, lanes], preferred_element_type=jnp.float32
            ) + jnp.dot(read[:, half:], powers[1][:, lanes], preferred_element_type=jnp.float32)
            total = summed[64:65]
            level = jnp.log2(total)
            if top is not None:
                level = level + top[:, lanes] * SCALE
            row = pl.ds(head + n, 1)
            mine = 1.0 / (1.0 + jnp.exp2(home[row, :] - level))
            mine = mine.astype(jnp.bfloat16).astype(jnp.float32)
            share[row, :] = mine
            found.append((summed[:64] * (mine / total), level))
        return found

    gathered = jnp.zeros(acc.shape, jnp.float32)
    levels = []
    ahead = scores_at(0)
    for head in range(0, heads, 2):
        scores = ahead
        if head + 2 < heads:
            ahead = scores_at((head + 2) * HD)
        for piece, level in finish(head, scores, None):
            gathered = gathered + piece
            levels.append(level)
    acc[...] = gathered

    @pl.when(jnp.logical_not(worst(levels) < SAFE))
    def _():
        acc[...] = jnp.zeros_like(acc)

        def body(n, carry):
            scores = scores_at(pl.multiple_of(n * 2 * HD, 2 * HD))
            top = jnp.maximum(*(jnp.max(s, axis=0, keepdims=True) for s in scores))
            for piece, _ in finish(2 * n, scores, top):
                acc[...] += piece
            return carry

        lax.fori_loop(0, heads // 2, body, 0)

    out[:64] = acc[...].astype(jnp.bfloat16)
    out[64:] = share[...].astype(jnp.bfloat16)


def blend(remote, mean, start):
    acc = remote[:64].astype(jnp.float32)
    for h in range(mean.shape[0]):
        keep = 1.0 - remote[64 + h : 65 + h].astype(jnp.float32)
        acc = acc + mean[h, :, start : start + acc.shape[1]] * keep
    return acc


def early_kernel(remote, mean, out):
    out[...] = blend(remote, mean, 0)


def merge_kernel(remote, mean, early, own, other):
    late = blend(remote, mean, early.shape[1])
    mixed = early[:, 256:]
    first = lax.broadcasted_iota(jnp.int32, late.shape, 1) < 64
    own[:, :128] = early[:, :128].astype(jnp.bfloat16)
    other[:, :128] = early[:, 128:256].astype(jnp.bfloat16)
    own[:, 128:] = jnp.where(first, mixed, pltpu.roll(late, 64, 1)).astype(jnp.bfloat16)
    other[:, 128:] = jnp.where(first, pltpu.roll(mixed, 64, 1), late).astype(jnp.bfloat16)


def prepare_kernel(
    me, grp, kinds, w0, w1, w2, w3, w_env, final, scale, shift, light,
    mixer, cross, direct, base, bias, reads, gram, column, sums, shifts,
):
    step = pl.program_id(0)
    lights = scale.shape[0]
    width = pl.num_programs(0) * w0.shape[1]

    @pl.when(step == 0)
    def _():
        for ref in (reads, gram, column, sums, shifts):
            ref[...] = jnp.zeros_like(ref)

    rows = jnp.concatenate((w0[...], w1[...], w2[...], w3[...], w_env[...]), axis=0)
    weight = final[...].astype(jnp.float32)

    def fold(block):
        total = block[:, :128]
        for s in range(1, block.shape[1] // 128):
            total = total + block[:, s * 128 : (s + 1) * 128]
        return total

    gains = []
    for l in range(lights):
        gained = weight * (1.0 + scale[l : l + 1, :].astype(jnp.float32))
        gains += split(gained)
        sums[l] = sums[l] + fold(gained)
        shifts[l] = shifts[l] + fold(weight * shift[l : l + 1, :].astype(jnp.float32))
    ones = jnp.ones((16, rows.shape[1]), jnp.bfloat16)
    reads[...] += dot_lanes(jnp.concatenate(gains + [ones], axis=0), rows)
    gram[...] += dot_lanes(rows, rows)
    column[...] += dot_lanes(rows, jnp.ones((128, rows.shape[1]), jnp.bfloat16))

    @pl.when(step == pl.num_programs(0) - 1)
    def _():
        average = reads[256:257] * (1.0 / width)
        centred = gram[...] * (1.0 / width) - (column[:, :1] * (1.0 / width)) * average
        mixer[:256], mixer[256:512] = split(centred[:256, :256])
        for l in range(lights):
            total = jnp.sum(sums[l], axis=1, keepdims=True)
            read = reads[l * 128 : l * 128 + 64] + reads[l * 128 + 64 : l * 128 + 128]
            read = read - total * average
            start = 512 + l * 128
            mixer[start : start + 64], mixer[start + 64 : start + 128] = split(read[:, :256])
            bias[l] = jnp.broadcast_to(
                jnp.sum(shifts[l], axis=1, keepdims=True), bias.shape[1:]
            )
            tokens = light[l]
            cross[l] = 2.0 * dot_split(centred[:256, 256:], tokens)
            direct[l] = dot_split(read[:, 256:], tokens)
            turned = tokens.astype(jnp.float32).T
            own = jnp.sum(dot_split(centred[256:, 256:], tokens) * turned, axis=0, keepdims=True)
            base[l] = jnp.broadcast_to(own, base.shape[1:])


def render_kernel(place, a0, a1, a2, a3, mixer, cross, direct, base, bias, attrs, rendered):
    me = place[0]
    attrs[pl.ds(me, 1)] = a0[...][None]
    attrs[pl.ds(1 - me, 1)] = a1[...][None]
    latents = jnp.concatenate((a0[...], a1[...], a2[...], a3[...]), axis=0)
    mixed = jnp.dot(mixer[...], latents, preferred_element_type=jnp.float32)
    square = mixed[:256] + mixed[256:512]
    wide = latents.astype(jnp.float32)
    for l in range(rendered.shape[0]):
        spread = jnp.sum(wide * (square + cross[l]), axis=0, keepdims=True) + base[l, :1]
        invert = lax.rsqrt(jnp.maximum(spread, 0.0) + EPS)
        start = 512 + l * 128
        read = mixed[start : start + 64] + mixed[start + 64 : start + 128] + direct[l]
        shift = jnp.concatenate([bias[l]] * (read.shape[1] // 128), axis=1)
        rendered[l] = (read * invert + shift).astype(jnp.bfloat16)


LIMIT = pltpu.CompilerParams(vmem_limit_bytes=24 << 20)
RESIDENT = pl.BlockSpec(memory_space=pltpu.VMEM)


def resident(*arrays):
    return [pltpu.with_memory_space_constraint(a, pltpu.VMEM) for a in arrays]


def stay(array):
    return pltpu.with_memory_space_constraint(array, pltpu.HBM)


def whole(shape):
    return pl.BlockSpec(shape, lambda *_: (0,) * len(shape))


def on_device(
    q_inv,
    k_inv,
    v_inv,
    group_ids,
    w_attr,
    env_ids,
    env_table,
    w_embed_attr,
    w_embed_env,
    mod_scale,
    mod_shift,
    w_final,
):
    groups, rows, width = q_inv.shape
    heads = width // HD
    first = 3 * rows // 4
    patch = w_attr.shape[2]
    lights, model = mod_scale.shape
    channels = w_embed_env.shape[0]
    me = lax.axis_index("seq") % 2
    grp = lax.axis_index("grp")

    place = me.reshape(1).astype(jnp.int32)
    side = grp.reshape(1).astype(jnp.int32)
    scalar = pl.BlockSpec(memory_space=pltpu.SMEM)
    remain = pl.BlockSpec(memory_space=pltpu.HBM)
    ahead, behind = pl.pallas_call(
        first_kernel,
        in_specs=[scalar, remain],
        out_specs=[RESIDENT] * 2,
        out_shape=[pltpu.VMEM((first, width), jnp.bfloat16)] * 2,
        scratch_shapes=[pltpu.SemaphoreType.DMA((2,))],
        compiler_params=LIMIT,
        name="first",
    )(place, stay(q_inv))
    same0 = seq_swap(ahead, 2)
    cross0 = seq_swap(behind, 3)
    late_same, late_cross, bundle = pl.pallas_call(
        second_kernel,
        in_specs=[scalar, remain, remain, remain],
        out_specs=[remain] * 3,
        out_shape=[
            pltpu.HBM((rows - first, width), jnp.bfloat16),
            pltpu.HBM((rows - first, width), jnp.bfloat16),
            pltpu.HBM((3, rows, width), jnp.bfloat16),
        ],
        scratch_shapes=[
            pltpu.VMEM((3, rows, width), jnp.bfloat16),
            pltpu.VMEM((2, rows - first, width), jnp.bfloat16),
        ]
        + [pltpu.SemaphoreType.DMA((5,))] * 2,
        compiler_params=LIMIT,
        name="second",
    )(place, stay(q_inv), stay(k_inv), stay(v_inv))
    bundle = seq_swap(bundle, 1)

    cols = STEP_HEADS * HD
    steps = heads // STEP_HEADS
    picked = pl.BlockSpec((None, rows, cols), lambda g, m, *_: (m[0], 0, g))
    given = [
        pl.BlockSpec((None, rows, cols), lambda g, *_, n=n: (n, 0, g)) for n in range(3)
    ]
    reads = pl.BlockSpec((STEP_HEADS, 80, 2 * rows), lambda g, *_: (g, 0, 0))
    vw, mean, level = pl.pallas_call(
        local_kernel,
        grid_spec=pltpu.PrefetchScalarGridSpec(
            num_scalar_prefetch=3,
            grid=(steps,),
            in_specs=[
                picked,
                given[0],
                picked,
                given[1],
                picked,
                given[2],
                pl.BlockSpec(
                    (None, patch, cols), lambda g, m, r, t: (t[2 * r[0] + m[0]], 0, g)
                ),
            ],
            out_specs=[
                reads,
                pl.BlockSpec((STEP_HEADS, 64, 2 * rows), lambda g, *_: (g, 0, 0)),
                whole((heads, 2 * rows)),
            ],
        ),
        out_shape=[
            jax.ShapeDtypeStruct((heads, 80, 2 * rows), jnp.bfloat16),
            jax.ShapeDtypeStruct((heads, 64, 2 * rows), jnp.float32),
            jax.ShapeDtypeStruct((heads, 2 * rows), jnp.float32),
        ],
        compiler_params=LIMIT,
        name="local",
    )(
        place,
        side,
        group_ids,
        stay(q_inv),
        bundle,
        stay(k_inv),
        bundle,
        stay(v_inv),
        bundle,
        stay(jnp.swapaxes(w_attr, 1, 2)),
    )

    level, late_same, late_cross = lax.optimization_barrier((level, late_same, late_cross))
    home = seq_swap(level, 2)
    same1 = seq_swap(late_same, 2)
    cross1 = seq_swap(late_cross, 3)

    lighting = jnp.take(env_table, env_ids, axis=0)
    strips = model // CHUNK
    weights = [
        pl.BlockSpec(
            (None, patch, CHUNK),
            lambda g, m, r, t, n=n: (
                t[2 * (r[0] if n < 2 else 1 - r[0]) + (1 - m[0] if n % 2 else m[0])],
                0,
                g,
            ),
        )
        for n in range(4)
    ]
    strip = lambda count: pl.BlockSpec((count, CHUNK), lambda g, *_: (0, g))
    kinds = 4 * patch
    inputs = kinds + channels
    out_shapes = [
        pltpu.VMEM((2 * kinds + 2 * lights * patch, kinds), jnp.bfloat16),
        pltpu.VMEM((lights, kinds, rows), jnp.float32),
        pltpu.VMEM((lights, patch, rows), jnp.float32),
        pltpu.VMEM((lights, 8, rows), jnp.float32),
        pltpu.VMEM((lights, patch, 128), jnp.float32),
    ]
    prepared = pl.pallas_call(
        prepare_kernel,
        grid_spec=pltpu.PrefetchScalarGridSpec(
            num_scalar_prefetch=3,
            grid=(strips,),
            in_specs=weights
            + [
                strip(channels),
                strip(patch),
                strip(lights),
                strip(lights),
                whole((lights, rows, channels)),
            ],
            out_specs=[whole(s.shape) for s in out_shapes],
            scratch_shapes=[
                pltpu.VMEM((2 * lights * patch + 16, inputs), jnp.float32),
                pltpu.VMEM((inputs, inputs), jnp.float32),
                pltpu.VMEM((inputs, 128), jnp.float32),
                pltpu.VMEM((lights, patch, 128), jnp.float32),
                pltpu.VMEM((lights, patch, 128), jnp.float32),
            ],
        ),
        out_shape=out_shapes,
        compiler_params=LIMIT,
        name="prepare",
    )(
        place,
        side,
        group_ids,
        w_embed_attr,
        w_embed_attr,
        w_embed_attr,
        w_embed_attr,
        w_embed_env,
        w_final.T,
        mod_scale,
        mod_shift,
        lighting,
    )

    def remote(same, crossed, spans, lane):
        count = same.shape[0]
        wide = 2 * count
        block = pl.BlockSpec((count, cols), lambda g, m: (0, g))
        sent = pl.pallas_call(
            lambda *refs: remote_kernel(spans, *refs),
            grid_spec=pltpu.PrefetchScalarGridSpec(
                num_scalar_prefetch=1,
                grid=(steps,),
                in_specs=[
                    block,
                    block,
                    picked,
                    given[1],
                    reads,
                    pl.BlockSpec((heads, wide), lambda g, m: (0, lane)),
                ],
                out_specs=whole((64 + heads, wide)),
                scratch_shapes=[
                    pltpu.VMEM((64, wide), jnp.float32),
                    pltpu.VMEM((heads, wide), jnp.float32),
                ],
            ),
            out_shape=jax.ShapeDtypeStruct((64 + heads, wide), jnp.bfloat16),
            compiler_params=LIMIT,
            name="remote",
        )(place, same, crossed, k_inv, bundle, vw, home)
        return seq_swap(sent, 2)

    back0 = remote(same0, cross0, ((0, 128), (128, 192)), 0)
    last = 2 * (rows - first)
    back1 = seq_swap(
        pl.pallas_call(
            last_kernel,
            in_specs=[scalar] + [RESIDENT] * 6,
            out_specs=RESIDENT,
            out_shape=pltpu.VMEM((64 + heads, last), jnp.bfloat16),
            scratch_shapes=[
                pltpu.VMEM((64, last), jnp.float32),
                pltpu.VMEM((heads, last), jnp.float32),
            ],
            compiler_params=LIMIT,
            name="last",
        )(place, *resident(same1, cross1, k_inv, bundle[1], vw, home[:, 2 * first :])),
        2,
    )
    early = pl.pallas_call(
        early_kernel,
        in_specs=[RESIDENT] * 2,
        out_specs=RESIDENT,
        out_shape=pltpu.VMEM((64, 2 * first), jnp.float32),
        compiler_params=LIMIT,
        name="early",
    )(*resident(back0, mean))
    own, other = pl.pallas_call(
        merge_kernel,
        in_specs=[RESIDENT] * 3,
        out_specs=[RESIDENT] * 2,
        out_shape=[pltpu.VMEM((64, rows), jnp.bfloat16)] * 2,
        compiler_params=LIMIT,
        name="merge",
    )(*resident(back1, mean, early))
    a1 = seq_swap(other, 1)
    a2 = grp_swap(own)
    a3 = both_swap(other)
    attrs, rendered = pl.pallas_call(
        render_kernel,
        in_specs=[pl.BlockSpec(memory_space=pltpu.SMEM)] + [RESIDENT] * 9,
        out_specs=[RESIDENT] * 2,
        out_shape=[
            jax.ShapeDtypeStruct((groups, patch, rows), jnp.bfloat16),
            jax.ShapeDtypeStruct((lights, patch, rows), jnp.bfloat16),
        ],
        compiler_params=LIMIT,
        name="render",
    )(place, *resident(own, a1, a2, a3, *prepared))
    return (jnp.swapaxes(attrs, 1, 2), jnp.swapaxes(rendered, 1, 2))


def solution(mesh):
    in_specs = (
        P("grp", "seq", None),
        P("grp", "seq", None),
        P("grp", "seq", None),
        P(),
        P(),
        P("grp", "seq"),
        P(),
        P(),
        P(),
        P("grp", None),
        P("grp", None),
        P(),
    )
    out_specs = (P("grp", "seq", None), P("grp", "seq", None))
    return jax.shard_map(
        on_device, mesh=mesh, in_specs=in_specs, out_specs=out_specs, check_vma=False
    )
```

```python
import math

import jax
import jax.numpy as jnp
from jax import lax
from jax.experimental import pallas as pl
from jax.experimental.pallas import tpu as pltpu
from jax.sharding import PartitionSpec as P


HD = 128
STEP_HEADS = 4
EPS = 1e-06
SCALE = HD ** (-0.5) * math.log2(math.e)
SAFE = 60.0
CHUNK = 1024
OVER_LANES = (((1,), (1,)), ((), ()))


def seq_swap(block, flip):
    count = lax.axis_size("seq")
    return lax.ppermute(block, "seq", [(i, i ^ flip) for i in range(count)])


def grp_swap(block):
    return lax.ppermute(block, "grp", [(0, 1), (1, 0)])


def both_swap(block, flip):
    count = lax.axis_size("seq")
    route = [
        (g * count + i, (1 - g) * count + (i ^ flip)) for g in range(2) for i in range(count)
    ]
    return lax.ppermute(block, ("grp", "seq"), route)


def dot_lanes(left, right):
    return lax.dot_general(left, right, OVER_LANES, preferred_element_type=jnp.float32)


def split(block):
    high = block.astype(jnp.bfloat16)
    return high, (block - high.astype(jnp.float32)).astype(jnp.bfloat16)


def dot_split(left, right):
    high, low = split(left)
    return dot_lanes(high, right) + dot_lanes(low, right)


def scores_of(keys, queries):
    half = keys.shape[0] // 2
    return [dot_lanes(keys[:half], queries), dot_lanes(keys[half:], queries)]


def plain_softmax(units):
    found = []
    ahead = scores_of(*units[0][:2])
    for n, (_, _, values) in enumerate(units):
        scores = ahead
        if n + 1 < len(units):
            ahead = scores_of(*units[n + 1][:2])
        half = values.shape[1] // 2
        powers = [jnp.exp2(s * SCALE).astype(jnp.bfloat16) for s in scores]
        summed = jnp.dot(
            values[:, :half], powers[0], preferred_element_type=jnp.float32
        ) + jnp.dot(values[:, half:], powers[1], preferred_element_type=jnp.float32)
        total = summed[64:65]
        found.append((summed[:64], total, jnp.log2(total)))
    return found


def shifted_softmax(units):
    found = []
    for keys, queries, values in units:
        scores = dot_lanes(keys, queries)
        top = jnp.max(scores, axis=0, keepdims=True)
        powers = jnp.exp2((scores - top) * SCALE).astype(jnp.bfloat16)
        summed = jnp.dot(values, powers, preferred_element_type=jnp.float32)
        total = summed[64:65]
        found.append((summed[:64], total, top * SCALE + jnp.log2(total)))
    return found


def worst(levels):
    largest = jnp.abs(levels[0])
    for level in levels[1:]:
        largest = jnp.maximum(largest, jnp.abs(level))
    return jnp.max(largest)


def shuttle(pieces, arrive, leave):
    inward = [
        pltpu.make_async_copy(source, held, arrive.at[n])
        for n, (source, held, _) in enumerate(pieces)
    ]
    outward = [
        pltpu.make_async_copy(held, target, leave.at[n])
        for n, (_, held, target) in enumerate(pieces)
    ]
    for copy in inward:
        copy.start()
    for here, there in zip(inward, outward):
        here.wait()
        there.start()
    for copy in outward:
        copy.wait()


def first_kernel(place, q, same, cross, arrive):
    me = place[0]
    rows = pl.ds(0, same.shape[0])
    copies = [
        pltpu.make_async_copy(q.at[me, rows], same, arrive.at[0]),
        pltpu.make_async_copy(q.at[1 - me, rows], cross, arrive.at[1]),
    ]
    for copy in copies:
        copy.start()
    for copy in copies:
        copy.wait()


def second_kernel(place, q, k, v, bundle, sb, cb, sc, cc, held, rest, arrive, leave):
    me = place[0]
    count = sb.shape[0]
    start = q.shape[1] - 2 * count
    pieces = [(a.at[1 - me], held.at[n], bundle.at[n]) for n, a in enumerate((q, k, v))]
    for n, (same, cross) in enumerate(((sb, cb), (sc, cc))):
        span = pl.ds(start + n * count, count)
        pieces.append((q.at[me, span], rest.at[2 * n], same))
        pieces.append((q.at[1 - me, span], rest.at[2 * n + 1], cross))
    shuttle(pieces, arrive, leave)


def local_kernel(me, grp, kinds, q, qx, k, kx, v, vx, w, vw, mean, own, part, level):
    step = pl.program_id(0)
    reads = []

    for i in range(STEP_HEADS):
        cols = slice(i * HD, (i + 1) * HD)
        values = jnp.concatenate((v[:, cols], vx[:, cols]), axis=0)
        read = dot_lanes(w[:, cols], values).astype(jnp.bfloat16)
        read = jnp.concatenate((read, jnp.ones((16, read.shape[1]), jnp.bfloat16)), axis=0)
        vw[i] = read
        reads.append(read)

    def attend(softmax):
        units = []
        for i in range(STEP_HEADS):
            cols = slice(i * HD, (i + 1) * HD)
            keys = jnp.concatenate((k[:, cols], kx[:, cols]), axis=0)
            for a, b in ((0, 128), (128, 256)):
                queries = jnp.concatenate((q[a:b, cols], qx[a:b, cols]), axis=0)
                units.append((keys, queries, reads[i]))
        found = softmax(units)
        levels = []
        for i in range(STEP_HEADS):
            rows = []
            for n in range(2):
                summed, total, row = found[2 * i + n]
                scaled = summed * (1.0 / total)
                if n == 0:
                    mean[i] = scaled
                else:
                    own[i] = scaled[:, :128].astype(jnp.bfloat16)
                    part[i] = scaled[:, 128:].astype(jnp.bfloat16)
                rows.append(row)
            levels.append(jnp.concatenate(rows, axis=1))
            level[pl.ds(step * STEP_HEADS + i, 1), :] = levels[-1]
        return worst(levels)

    reach = attend(plain_softmax)

    @pl.when(jnp.logical_not(reach < SAFE))
    def _():
        attend(shifted_softmax)


def remote_kernel(spans, me, qs, qd, k, kx, vw, home, out, acc, share):
    step = pl.program_id(0)

    @pl.when(step == 0)
    def _():
        acc[...] = jnp.zeros_like(acc)

    before = acc[...]

    def attend(softmax):
        gathered = [before[:, a * 2 : b * 2] for a, b in spans]
        units = []
        for i in range(STEP_HEADS):
            cols = slice(i * HD, (i + 1) * HD)
            keys = jnp.concatenate((k[:, cols], kx[:, cols]), axis=0)
            for a, b in spans:
                queries = jnp.concatenate((qs[a:b, cols], qd[a:b, cols]), axis=0)
                units.append((keys, queries, vw[i]))
        found = softmax(units)
        levels = []
        for i in range(STEP_HEADS):
            row = pl.ds(step * STEP_HEADS + i, 1)
            theirs = home[row, :]
            rows, mines = [], []
            for n, (a, b) in enumerate(spans):
                summed, total, level = found[i * len(spans) + n]
                mine = 1.0 / (1.0 + jnp.exp2(theirs[:, 2 * a : 2 * b] - level))
                mine = mine.astype(jnp.bfloat16).astype(jnp.float32)
                gathered[n] = gathered[n] + summed * (mine / total)
                mines.append(mine)
                rows.append(level)
            share[row, :] = jnp.concatenate(mines, axis=1)
            levels.append(jnp.concatenate(rows, axis=1))
        for n, (a, b) in enumerate(spans):
            acc[:, 2 * a : 2 * b] = gathered[n]
        return worst(levels)

    reach = attend(plain_softmax)

    @pl.when(jnp.logical_not(reach < SAFE))
    def _():
        attend(shifted_softmax)

    @pl.when(step == pl.num_programs(0) - 1)
    def _():
        out[:64] = acc[...].astype(jnp.bfloat16)
        out[64:] = share[...].astype(jnp.bfloat16)


def halves(left, right):
    first = lax.broadcasted_iota(jnp.int32, left.shape, 1) < 64
    return (
        jnp.where(first, left, pltpu.roll(right, 64, 1)),
        jnp.where(first, pltpu.roll(left, 64, 1), right),
    )


def last_kernel(phase, place, qs, qd, k, kx, vw, home, *refs):
    prior, outs, (acc, share, near) = refs[:phase], refs[phase:-3], refs[-3:]
    me = place[0]
    heads = vw.shape[0]
    near[...] = halves(home[:, 256:384], home[:, 384:512])[phase]
    zero = jnp.zeros((2 * qs.shape[0], HD), jnp.bfloat16)

    def scores_at(start):
        cols = pl.ds(start, 2 * HD)
        keys = jnp.concatenate((k[me, :, cols], kx[:, cols]), axis=0)
        pair = jnp.concatenate((qs[:, cols], qd[:, cols]), axis=0)
        queries = jnp.concatenate(
            (
                jnp.concatenate((pair[:, :HD], zero), axis=1),
                jnp.concatenate((zero, pair[:, HD:]), axis=1),
            ),
            axis=0,
        )
        half = keys.shape[0] // 2
        return [dot_lanes(keys[:half], queries), dot_lanes(keys[half:], queries)]

    def finish(head, scores, top):
        wide = scores[0].shape[1] // 2
        powers = []
        for block in scores:
            shifted = block if top is None else block - top
            powers.append(jnp.exp2(shifted * SCALE).astype(jnp.bfloat16))
        found = []
        for n in range(2):
            read = vw[head + n]
            half = read.shape[1] // 2
            lanes = slice(n * wide, (n + 1) * wide)
            summed = jnp.dot(
                read[:, :half], powers[0][:, lanes], preferred_element_type=jnp.float32
            ) + jnp.dot(read[:, half:], powers[1][:, lanes], preferred_element_type=jnp.float32)
            total = summed[64:65]
            level = jnp.log2(total)
            if top is not None:
                level = level + top[:, lanes] * SCALE
            row = pl.ds(head + n, 1)
            mine = 1.0 / (1.0 + jnp.exp2(near[row, :] - level))
            mine = mine.astype(jnp.bfloat16).astype(jnp.float32)
            share[row, :] = mine
            found.append((summed[:64] * (mine / total), level))
        return found

    gathered = jnp.zeros(acc.shape, jnp.float32)
    levels = []
    ahead = scores_at(0)
    for head in range(0, heads, 2):
        scores = ahead
        if head + 2 < heads:
            ahead = scores_at((head + 2) * HD)
        for piece, level in finish(head, scores, None):
            gathered = gathered + piece
            levels.append(level)
    acc[...] = gathered

    @pl.when(jnp.logical_not(worst(levels) < SAFE))
    def _():
        acc[...] = jnp.zeros_like(acc)

        def body(n, carry):
            scores = scores_at(pl.multiple_of(n * 2 * HD, 2 * HD))
            top = jnp.maximum(*(jnp.max(s, axis=0, keepdims=True) for s in scores))
            for piece, _ in finish(2 * n, scores, top):
                acc[...] += piece
            return carry

        lax.fori_loop(0, heads // 2, body, 0)

    if phase == 0:
        outs[0][:64] = acc[...]
        outs[0][64:] = share[...]
    else:
        for a, b, now in ((0, 64, acc), (64, 64 + heads, share)):
            own, part = halves(prior[0][a:b], now[...])
            outs[0][a:b] = own.astype(jnp.bfloat16)
            outs[1][a:b] = part.astype(jnp.bfloat16)


def blend(remote, mean):
    acc = remote[:64].astype(jnp.float32)
    for h in range(mean.shape[0]):
        keep = 1.0 - remote[64 + h : 65 + h].astype(jnp.float32)
        acc = acc + mean[h].astype(jnp.float32) * keep
    return acc.astype(jnp.bfloat16)


def join_kernel(remote, mean, own, other):
    found = blend(remote, mean)
    half = found.shape[1] // 2
    own[...] = found[:, :half]
    other[...] = found[:, half:]


def prepare_kernel(
    me, grp, kinds, w0, w1, w2, w3, w_env, final, scale, shift, light,
    mixer, cross, direct, base, bias, reads, gram, column, sums, shifts,
):
    step = pl.program_id(0)
    lights = scale.shape[0]
    width = pl.num_programs(0) * w0.shape[1]

    @pl.when(step == 0)
    def _():
        for ref in (reads, gram, column, sums, shifts):
            ref[...] = jnp.zeros_like(ref)

    rows = jnp.concatenate((w0[...], w1[...], w2[...], w3[...], w_env[...]), axis=0)
    weight = final[...].astype(jnp.float32)

    def fold(block):
        total = block[:, :128]
        for s in range(1, block.shape[1] // 128):
            total = total + block[:, s * 128 : (s + 1) * 128]
        return total

    gains = []
    for l in range(lights):
        gained = weight * (1.0 + scale[l : l + 1, :].astype(jnp.float32))
        gains += split(gained)
        sums[l] = sums[l] + fold(gained)
        shifts[l] = shifts[l] + fold(weight * shift[l : l + 1, :].astype(jnp.float32))
    ones = jnp.ones((16, rows.shape[1]), jnp.bfloat16)
    reads[...] += dot_lanes(jnp.concatenate(gains + [ones], axis=0), rows)
    gram[...] += dot_lanes(rows, rows)
    column[...] += dot_lanes(rows, jnp.ones((128, rows.shape[1]), jnp.bfloat16))

    @pl.when(step == pl.num_programs(0) - 1)
    def _():
        average = reads[256:257] * (1.0 / width)
        centred = gram[...] * (1.0 / width) - (column[:, :1] * (1.0 / width)) * average
        mixer[:256], mixer[256:512] = split(centred[:256, :256])
        for l in range(lights):
            total = jnp.sum(sums[l], axis=1, keepdims=True)
            read = reads[l * 128 : l * 128 + 64] + reads[l * 128 + 64 : l * 128 + 128]
            read = read - total * average
            start = 512 + l * 128
            mixer[start : start + 64], mixer[start + 64 : start + 128] = split(read[:, :256])
            bias[l] = jnp.broadcast_to(
                jnp.sum(shifts[l], axis=1, keepdims=True), bias.shape[1:]
            )
            tokens = light[l]
            cross[l] = 2.0 * dot_split(centred[:256, 256:], tokens)
            direct[l] = dot_split(read[:, 256:], tokens)
            turned = tokens.astype(jnp.float32).T
            own = jnp.sum(dot_split(centred[256:, 256:], tokens) * turned, axis=0, keepdims=True)
            base[l] = jnp.broadcast_to(own, base.shape[1:])


def render_kernel(place, *refs):
    ready, remote, mean = refs[:4], refs[4:8], refs[8:12]
    mixer, cross, direct, base, bias, attrs, rendered = refs[12:]
    me = place[0]
    found = [
        jnp.concatenate((a[...], blend(r, m)), axis=1) for a, r, m in zip(ready, remote, mean)
    ]
    attrs[pl.ds(me, 1)] = found[0][None]
    attrs[pl.ds(1 - me, 1)] = found[1][None]
    latents = jnp.concatenate(found, axis=0)
    mixed = jnp.dot(mixer[...], latents, preferred_element_type=jnp.float32)
    square = mixed[:256] + mixed[256:512]
    wide = latents.astype(jnp.float32)
    for l in range(rendered.shape[0]):
        spread = jnp.sum(wide * (square + cross[l]), axis=0, keepdims=True) + base[l, :1]
        invert = lax.rsqrt(jnp.maximum(spread, 0.0) + EPS)
        start = 512 + l * 128
        read = mixed[start : start + 64] + mixed[start + 64 : start + 128] + direct[l]
        shift = jnp.concatenate([bias[l]] * (read.shape[1] // 128), axis=1)
        rendered[l] = (read * invert + shift).astype(jnp.bfloat16)


LIMIT = pltpu.CompilerParams(vmem_limit_bytes=14 << 20)
RESIDENT = pl.BlockSpec(memory_space=pltpu.VMEM)


def resident(*arrays):
    return [pltpu.with_memory_space_constraint(a, pltpu.VMEM) for a in arrays]


def stay(array):
    return pltpu.with_memory_space_constraint(array, pltpu.HBM)


def whole(shape):
    return pl.BlockSpec(shape, lambda *_: (0,) * len(shape))


def on_device(
    q_inv,
    k_inv,
    v_inv,
    group_ids,
    w_attr,
    env_ids,
    env_table,
    w_embed_attr,
    w_embed_env,
    mod_scale,
    mod_shift,
    w_final,
):
    groups, rows, width = q_inv.shape
    heads = width // HD
    first = rows // 2
    piece = rows // 4
    patch = w_attr.shape[2]
    lights, model = mod_scale.shape
    channels = w_embed_env.shape[0]
    me = lax.axis_index("seq") % 2
    grp = lax.axis_index("grp")

    place = me.reshape(1).astype(jnp.int32)
    side = grp.reshape(1).astype(jnp.int32)
    scalar = pl.BlockSpec(memory_space=pltpu.SMEM)
    remain = pl.BlockSpec(memory_space=pltpu.HBM)
    ahead, behind = pl.pallas_call(
        first_kernel,
        in_specs=[scalar, remain],
        out_specs=[RESIDENT] * 2,
        out_shape=[pltpu.VMEM((first, width), jnp.bfloat16)] * 2,
        scratch_shapes=[pltpu.SemaphoreType.DMA((2,))],
        compiler_params=LIMIT,
        name="first",
    )(place, stay(q_inv))
    same0 = seq_swap(ahead, 2)
    cross0 = seq_swap(behind, 3)
    bundle, same1, cross1, same2, cross2 = pl.pallas_call(
        second_kernel,
        in_specs=[scalar, remain, remain, remain],
        out_specs=[remain] * 5,
        out_shape=[pltpu.HBM((3, rows, width), jnp.bfloat16)]
        + [pltpu.HBM((piece, width), jnp.bfloat16)] * 4,
        scratch_shapes=[
            pltpu.VMEM((3, rows, width), jnp.bfloat16),
            pltpu.VMEM((4, piece, width), jnp.bfloat16),
        ]
        + [pltpu.SemaphoreType.DMA((7,))] * 2,
        compiler_params=LIMIT,
        name="second",
    )(place, stay(q_inv), stay(k_inv), stay(v_inv))
    bundle = seq_swap(bundle, 1)

    cols = STEP_HEADS * HD
    steps = heads // STEP_HEADS
    picked = pl.BlockSpec((None, rows, cols), lambda g, m, *_: (m[0], 0, g))
    given = [
        pl.BlockSpec((None, rows, cols), lambda g, *_, n=n: (n, 0, g)) for n in range(3)
    ]
    reads = pl.BlockSpec((STEP_HEADS, 80, 2 * rows), lambda g, *_: (g, 0, 0))
    vw, mean, mean_own, mean_part, level = pl.pallas_call(
        local_kernel,
        grid_spec=pltpu.PrefetchScalarGridSpec(
            num_scalar_prefetch=3,
            grid=(steps,),
            in_specs=[
                picked,
                given[0],
                picked,
                given[1],
                picked,
                given[2],
                pl.BlockSpec(
                    (None, patch, cols), lambda g, m, r, t: (t[2 * r[0] + m[0]], 0, g)
                ),
            ],
            out_specs=[
                reads,
                pl.BlockSpec((STEP_HEADS, 64, rows), lambda g, *_: (g, 0, 0)),
                pl.BlockSpec((STEP_HEADS, 64, first), lambda g, *_: (g, 0, 0)),
                pl.BlockSpec((STEP_HEADS, 64, first), lambda g, *_: (g, 0, 0)),
                whole((heads, 2 * rows)),
            ],
        ),
        out_shape=[
            jax.ShapeDtypeStruct((heads, 80, 2 * rows), jnp.bfloat16),
            jax.ShapeDtypeStruct((heads, 64, rows), jnp.float32),
            jax.ShapeDtypeStruct((heads, 64, first), jnp.bfloat16),
            jax.ShapeDtypeStruct((heads, 64, first), jnp.bfloat16),
            jax.ShapeDtypeStruct((heads, 2 * rows), jnp.float32),
        ],
        compiler_params=LIMIT,
        name="local",
    )(
        place,
        side,
        group_ids,
        stay(q_inv),
        bundle,
        stay(k_inv),
        bundle,
        stay(v_inv),
        bundle,
        stay(jnp.swapaxes(w_attr, 1, 2)),
    )

    level, same1, cross1 = lax.optimization_barrier((level, same1, cross1))
    home = seq_swap(level, 2)
    same1 = seq_swap(same1, 2)
    cross1 = seq_swap(cross1, 3)
    means = [
        mean_own,
        seq_swap(mean_part, 1),
        grp_swap(mean_own),
        both_swap(mean_part, 1),
    ]
    kx = bundle[1]

    lighting = jnp.take(env_table, env_ids, axis=0)
    strips = model // CHUNK
    weights = [
        pl.BlockSpec(
            (None, patch, CHUNK),
            lambda g, m, r, t, n=n: (
                t[2 * (r[0] if n < 2 else 1 - r[0]) + (1 - m[0] if n % 2 else m[0])],
                0,
                g,
            ),
        )
        for n in range(4)
    ]
    strip = lambda count: pl.BlockSpec((count, CHUNK), lambda g, *_: (0, g))
    kinds = 4 * patch
    inputs = kinds + channels
    out_shapes = [
        pltpu.VMEM((2 * kinds + 2 * lights * patch, kinds), jnp.bfloat16),
        pltpu.VMEM((lights, kinds, rows), jnp.float32),
        pltpu.VMEM((lights, patch, rows), jnp.float32),
        pltpu.VMEM((lights, 8, rows), jnp.float32),
        pltpu.VMEM((lights, patch, 128), jnp.float32),
    ]
    prepared = pl.pallas_call(
        prepare_kernel,
        grid_spec=pltpu.PrefetchScalarGridSpec(
            num_scalar_prefetch=3,
            grid=(strips,),
            in_specs=weights
            + [
                strip(channels),
                strip(patch),
                strip(lights),
                strip(lights),
                whole((lights, rows, channels)),
            ],
            out_specs=[whole(s.shape) for s in out_shapes],
            scratch_shapes=[
                pltpu.VMEM((2 * lights * patch + 16, inputs), jnp.float32),
                pltpu.VMEM((inputs, inputs), jnp.float32),
                pltpu.VMEM((inputs, 128), jnp.float32),
                pltpu.VMEM((lights, patch, 128), jnp.float32),
                pltpu.VMEM((lights, patch, 128), jnp.float32),
            ],
        ),
        out_shape=out_shapes,
        compiler_params=LIMIT,
        name="prepare",
    )(
        place,
        side,
        group_ids,
        w_embed_attr,
        w_embed_attr,
        w_embed_attr,
        w_embed_attr,
        w_embed_env,
        w_final.T,
        mod_scale,
        mod_shift,
        lighting,
    )

    def remote(same, crossed, spans, lane):
        count = same.shape[0]
        wide = 2 * count
        block = pl.BlockSpec((count, cols), lambda g, m: (0, g))
        sent = pl.pallas_call(
            lambda *refs: remote_kernel(spans, *refs),
            grid_spec=pltpu.PrefetchScalarGridSpec(
                num_scalar_prefetch=1,
                grid=(steps,),
                in_specs=[
                    block,
                    block,
                    picked,
                    given[1],
                    reads,
                    pl.BlockSpec((heads, wide), lambda g, m: (0, lane)),
                ],
                out_specs=whole((64 + heads, wide)),
                scratch_shapes=[
                    pltpu.VMEM((64, wide), jnp.float32),
                    pltpu.VMEM((heads, wide), jnp.float32),
                ],
            ),
            out_shape=jax.ShapeDtypeStruct((64 + heads, wide), jnp.bfloat16),
            compiler_params=LIMIT,
            name="remote",
        )(place, same, crossed, k_inv, bundle, vw, home)
        return sent

    back0 = remote(same0, cross0, ((0, first),), 0)
    back0, same2, cross2 = lax.optimization_barrier((back0, same2, cross2))
    back0 = seq_swap(back0, 2)
    same2 = seq_swap(same2, 2)
    cross2 = seq_swap(cross2, 3)

    def attend(phase, same, crossed, *prior):
        shapes = [((64 + heads, first), jnp.bfloat16 if phase else jnp.float32)] * (1 + phase)
        return pl.pallas_call(
            lambda *refs: last_kernel(phase, *refs),
            in_specs=[scalar] + [RESIDENT] * (6 + phase),
            out_specs=[RESIDENT] * (1 + phase),
            out_shape=[pltpu.VMEM(*shape) for shape in shapes],
            scratch_shapes=[
                pltpu.VMEM((64, first), jnp.float32),
                pltpu.VMEM((heads, first), jnp.float32),
                pltpu.VMEM((heads, first), jnp.float32),
            ],
            compiler_params=LIMIT,
            name="last",
        )(place, *resident(same, crossed, k_inv, kx, vw, home, *prior))

    (prior,) = attend(0, same1, cross1)
    own, other = pl.pallas_call(
        join_kernel,
        in_specs=[RESIDENT] * 2,
        out_specs=[RESIDENT] * 2,
        out_shape=[pltpu.VMEM((64, first), jnp.bfloat16)] * 2,
        compiler_params=LIMIT,
        name="join",
    )(*resident(back0, mean))
    ready = [own, seq_swap(other, 1), grp_swap(own), both_swap(other, 1)]
    sent, passed = attend(1, same2, cross2, prior)
    parts = [
        seq_swap(sent, 2),
        seq_swap(passed, 3),
        both_swap(sent, 2),
        both_swap(passed, 3),
    ]
    attrs, rendered = pl.pallas_call(
        render_kernel,
        in_specs=[scalar] + [RESIDENT] * 17,
        out_specs=[RESIDENT] * 2,
        out_shape=[
            jax.ShapeDtypeStruct((groups, patch, rows), jnp.bfloat16),
            jax.ShapeDtypeStruct((lights, patch, rows), jnp.bfloat16),
        ],
        compiler_params=LIMIT,
        name="render",
    )(place, *resident(*ready, *parts, *means, *prepared))
    return (jnp.swapaxes(attrs, 1, 2), jnp.swapaxes(rendered, 1, 2))


def solution(mesh):
    in_specs = (
        P("grp", "seq", None),
        P("grp", "seq", None),
        P("grp", "seq", None),
        P(),
        P(),
        P("grp", "seq"),
        P(),
        P(),
        P(),
        P("grp", None),
        P("grp", None),
        P(),
    )
    out_specs = (P("grp", "seq", None), P("grp", "seq", None))
    return jax.shard_map(
        on_device, mesh=mesh, in_specs=in_specs, out_specs=out_specs, check_vma=False
    )
```

```python
import math

import jax
import jax.numpy as jnp
from jax import lax
from jax.experimental import pallas as pl
from jax.experimental.pallas import tpu as pltpu
from jax.sharding import PartitionSpec as P


HD = 128
STEP_HEADS = 4
EPS = 1e-06
SCALE = HD ** (-0.5) * math.log2(math.e)
SAFE = 60.0
CHUNK = 1024
OVER_LANES = (((1,), (1,)), ((), ()))


def seq_swap(block, flip):
    count = lax.axis_size("seq")
    return lax.ppermute(block, "seq", [(i, i ^ flip) for i in range(count)])


def grp_swap(block):
    return lax.ppermute(block, "grp", [(0, 1), (1, 0)])


def both_swap(block, flip):
    count = lax.axis_size("seq")
    route = [
        (g * count + i, (1 - g) * count + (i ^ flip)) for g in range(2) for i in range(count)
    ]
    return lax.ppermute(block, ("grp", "seq"), route)


def dot_lanes(left, right):
    return lax.dot_general(left, right, OVER_LANES, preferred_element_type=jnp.float32)


def split(block):
    high = block.astype(jnp.bfloat16)
    return high, (block - high.astype(jnp.float32)).astype(jnp.bfloat16)


def dot_split(left, right):
    high, low = split(left)
    return dot_lanes(high, right) + dot_lanes(low, right)


def scores_of(keys, queries):
    half = keys.shape[0] // 2
    return [dot_lanes(keys[:half], queries), dot_lanes(keys[half:], queries)]


def plain_softmax(units):
    found = []
    ahead = scores_of(*units[0][:2])
    for n, (_, _, values) in enumerate(units):
        scores = ahead
        if n + 1 < len(units):
            ahead = scores_of(*units[n + 1][:2])
        half = values.shape[1] // 2
        powers = [jnp.exp2(s * SCALE).astype(jnp.bfloat16) for s in scores]
        summed = jnp.dot(
            values[:, :half], powers[0], preferred_element_type=jnp.float32
        ) + jnp.dot(values[:, half:], powers[1], preferred_element_type=jnp.float32)
        total = summed[64:65]
        found.append((summed[:64], total, jnp.log2(total)))
    return found


def shifted_softmax(units):
    found = []
    for keys, queries, values in units:
        scores = dot_lanes(keys, queries)
        top = jnp.max(scores, axis=0, keepdims=True)
        powers = jnp.exp2((scores - top) * SCALE).astype(jnp.bfloat16)
        summed = jnp.dot(values, powers, preferred_element_type=jnp.float32)
        total = summed[64:65]
        found.append((summed[:64], total, top * SCALE + jnp.log2(total)))
    return found


def worst(levels):
    largest = jnp.abs(levels[0])
    for level in levels[1:]:
        largest = jnp.maximum(largest, jnp.abs(level))
    return jnp.max(largest)


def shuttle(pieces, arrive, leave):
    inward = [
        pltpu.make_async_copy(source, held, arrive.at[n])
        for n, (source, held, _) in enumerate(pieces)
    ]
    outward = [
        pltpu.make_async_copy(held, target, leave.at[n])
        for n, (_, held, target) in enumerate(pieces)
    ]
    for copy in inward:
        copy.start()
    for here, there in zip(inward, outward):
        here.wait()
        there.start()
    for copy in outward:
        copy.wait()


def first_kernel(place, q, same, cross, arrive):
    me = place[0]
    rows = pl.ds(0, same.shape[0])
    copies = [
        pltpu.make_async_copy(q.at[me, rows], same, arrive.at[0]),
        pltpu.make_async_copy(q.at[1 - me, rows], cross, arrive.at[1]),
    ]
    for copy in copies:
        copy.start()
    for copy in copies:
        copy.wait()


def second_kernel(place, q, k, v, bundle, sb, cb, s1, c1, s2, c2, held, rest, arrive, leave):
    me = place[0]
    count, width = sb.shape
    start = q.shape[1] - 2 * count
    left, right = pl.ds(0, width // 2), pl.ds(width // 2, width // 2)
    pieces = [(a.at[1 - me], held.at[n], bundle.at[n]) for n, a in enumerate((q, k, v))]
    for n, group, same, first, later in ((0, me, sb, s1, s2), (1, 1 - me, cb, c1, c2)):
        span = pl.ds(start, count)
        pieces.append((q.at[group, span], rest.at[n], same))
        span = pl.ds(start + count, count)
        for cols, target in ((left, first), (right, later)):
            pieces.append((q.at[group, span, cols], rest.at[2 + n, :, cols], target))
    shuttle(pieces, arrive, leave)


def local_kernel(me, grp, kinds, q, qx, k, kx, v, vx, w, vw, mean, own, part, level):
    step = pl.program_id(0)
    reads = []

    for i in range(STEP_HEADS):
        cols = slice(i * HD, (i + 1) * HD)
        values = jnp.concatenate((v[:, cols], vx[:, cols]), axis=0)
        read = dot_lanes(w[:, cols], values).astype(jnp.bfloat16)
        read = jnp.concatenate((read, jnp.ones((16, read.shape[1]), jnp.bfloat16)), axis=0)
        vw[i] = read
        reads.append(read)

    def attend(softmax):
        units = []
        for i in range(STEP_HEADS):
            cols = slice(i * HD, (i + 1) * HD)
            keys = jnp.concatenate((k[:, cols], kx[:, cols]), axis=0)
            for a, b in ((0, 128), (128, 256)):
                queries = jnp.concatenate((q[a:b, cols], qx[a:b, cols]), axis=0)
                units.append((keys, queries, reads[i]))
        found = softmax(units)
        levels = []
        for i in range(STEP_HEADS):
            rows = []
            for n in range(2):
                summed, total, row = found[2 * i + n]
                scaled = summed * (1.0 / total)
                if n == 0:
                    mean[i] = scaled
                else:
                    own[i] = scaled[:, :128].astype(jnp.bfloat16)
                    part[i] = scaled[:, 128:].astype(jnp.bfloat16)
                rows.append(row)
            levels.append(jnp.concatenate(rows, axis=1))
            level[pl.ds(step * STEP_HEADS + i, 1), :] = levels[-1]
        return worst(levels)

    reach = attend(plain_softmax)

    @pl.when(jnp.logical_not(reach < SAFE))
    def _():
        attend(shifted_softmax)


def remote_kernel(spans, me, qs, qd, k, kx, vw, home, out, acc, share):
    step = pl.program_id(0)

    @pl.when(step == 0)
    def _():
        acc[...] = jnp.zeros_like(acc)

    before = acc[...]

    def attend(softmax):
        gathered = [before[:, a * 2 : b * 2] for a, b in spans]
        units = []
        for i in range(STEP_HEADS):
            cols = slice(i * HD, (i + 1) * HD)
            keys = jnp.concatenate((k[:, cols], kx[:, cols]), axis=0)
            for a, b in spans:
                queries = jnp.concatenate((qs[a:b, cols], qd[a:b, cols]), axis=0)
                units.append((keys, queries, vw[i]))
        found = softmax(units)
        levels = []
        for i in range(STEP_HEADS):
            row = pl.ds(step * STEP_HEADS + i, 1)
            theirs = home[row, :]
            rows, mines = [], []
            for n, (a, b) in enumerate(spans):
                summed, total, level = found[i * len(spans) + n]
                mine = 1.0 / (1.0 + jnp.exp2(theirs[:, 2 * a : 2 * b] - level))
                mine = mine.astype(jnp.bfloat16).astype(jnp.float32)
                gathered[n] = gathered[n] + summed * (mine / total)
                mines.append(mine)
                rows.append(level)
            share[row, :] = jnp.concatenate(mines, axis=1)
            levels.append(jnp.concatenate(rows, axis=1))
        for n, (a, b) in enumerate(spans):
            acc[:, 2 * a : 2 * b] = gathered[n]
        return worst(levels)

    reach = attend(plain_softmax)

    @pl.when(jnp.logical_not(reach < SAFE))
    def _():
        attend(shifted_softmax)

    @pl.when(step == pl.num_programs(0) - 1)
    def _():
        out[:64] = acc[...].astype(jnp.bfloat16)
        out[64:] = share[...].astype(jnp.bfloat16)


def halves(left, right):
    first = lax.broadcasted_iota(jnp.int32, left.shape, 1) < 64
    return (
        jnp.where(first, left, pltpu.roll(right, 64, 1)),
        jnp.where(first, pltpu.roll(left, 64, 1), right),
    )


def last_kernel(stage, place, qs, qd, k, kx, vw, home, *refs):
    prior, outs, (acc, share, near) = refs[:stage], refs[stage:-3], refs[-3:]
    me = place[0]
    base = vw.shape[0] // 2 if stage == 2 else 0
    heads = base + qs.shape[1] // HD
    near[...] = halves(home[:, 256:384], home[:, 384:512])[1 if stage else 0]
    zero = jnp.zeros((2 * qs.shape[0], HD), jnp.bfloat16)
    if stage == 2:
        seed = prior[1][:64]
        share[:base] = prior[1][64 : 64 + base]
    else:
        seed = jnp.zeros(acc.shape, jnp.float32)

    def scores_at(head):
        cols = pl.ds(head * HD, 2 * HD)
        near_cols = pl.ds((head - base) * HD, 2 * HD)
        if not isinstance(head, int):
            cols = pl.ds(pl.multiple_of(head * HD, 2 * HD), 2 * HD)
            near_cols = pl.ds(pl.multiple_of((head - base) * HD, 2 * HD), 2 * HD)
        keys = jnp.concatenate((k[me, :, cols], kx[:, cols]), axis=0)
        pair = jnp.concatenate((qs[:, near_cols], qd[:, near_cols]), axis=0)
        queries = jnp.concatenate(
            (
                jnp.concatenate((pair[:, :HD], zero), axis=1),
                jnp.concatenate((zero, pair[:, HD:]), axis=1),
            ),
            axis=0,
        )
        half = keys.shape[0] // 2
        return [dot_lanes(keys[:half], queries), dot_lanes(keys[half:], queries)]

    def finish(head, scores, top):
        wide = scores[0].shape[1] // 2
        powers = []
        for block in scores:
            shifted = block if top is None else block - top
            powers.append(jnp.exp2(shifted * SCALE).astype(jnp.bfloat16))
        found = []
        for n in range(2):
            read = vw[head + n]
            half = read.shape[1] // 2
            lanes = slice(n * wide, (n + 1) * wide)
            summed = jnp.dot(
                read[:, :half], powers[0][:, lanes], preferred_element_type=jnp.float32
            ) + jnp.dot(read[:, half:], powers[1][:, lanes], preferred_element_type=jnp.float32)
            total = summed[64:65]
            level = jnp.log2(total)
            if top is not None:
                level = level + top[:, lanes] * SCALE
            row = pl.ds(head + n, 1)
            mine = 1.0 / (1.0 + jnp.exp2(near[row, :] - level))
            mine = mine.astype(jnp.bfloat16).astype(jnp.float32)
            share[row, :] = mine
            found.append((summed[:64] * (mine / total), level))
        return found

    gathered = seed
    levels = []
    ahead = scores_at(base)
    for head in range(base, heads, 2):
        scores = ahead
        if head + 2 < heads:
            ahead = scores_at(head + 2)
        for piece, level in finish(head, scores, None):
            gathered = gathered + piece
            levels.append(level)
    acc[...] = gathered

    @pl.when(jnp.logical_not(worst(levels) < SAFE))
    def _():
        acc[...] = seed

        def body(n, carry):
            scores = scores_at(base + 2 * n)
            top = jnp.maximum(*(jnp.max(s, axis=0, keepdims=True) for s in scores))
            for piece, _ in finish(base + 2 * n, scores, top):
                acc[...] += piece
            return carry

        lax.fori_loop(0, (heads - base) // 2, body, 0)

    if stage < 2:
        outs[0][:64] = acc[...]
        outs[0][64 : 64 + heads] = share[:heads]
    else:
        for a, b, now in ((0, 64, acc), (64, 64 + heads, share)):
            own, part = halves(prior[0][a:b], now[...])
            outs[0][a:b] = own.astype(jnp.bfloat16)
            outs[1][a:b] = part.astype(jnp.bfloat16)


def blend(remote, mean):
    acc = remote[:64].astype(jnp.float32)
    for h in range(mean.shape[0]):
        keep = 1.0 - remote[64 + h : 65 + h].astype(jnp.float32)
        acc = acc + mean[h].astype(jnp.float32) * keep
    return acc.astype(jnp.bfloat16)


def join_kernel(remote, mean, own, other):
    found = blend(remote, mean)
    half = found.shape[1] // 2
    own[...] = found[:, :half]
    other[...] = found[:, half:]


def begin_kernel(me, grp, kinds, w0, w1, w2, w3, w_env, final, scale, shift, *sums):
    @pl.when(pl.program_id(0) == 0)
    def _():
        for ref in sums:
            ref[...] = jnp.zeros_like(ref)

    gather_weights(w0, w1, w2, w3, w_env, final, scale, shift, *sums)


def gather_weights(w0, w1, w2, w3, w_env, final, scale, shift, reads, gram, column, sums, shifts):
    lights = scale.shape[0]
    rows = jnp.concatenate((w0[...], w1[...], w2[...], w3[...], w_env[...]), axis=0)
    weight = final[...].astype(jnp.float32)

    def fold(block):
        total = block[:, :128]
        for s in range(1, block.shape[1] // 128):
            total = total + block[:, s * 128 : (s + 1) * 128]
        return total

    gains = []
    for l in range(lights):
        gained = weight * (1.0 + scale[l : l + 1, :].astype(jnp.float32))
        gains += split(gained)
        sums[l] = sums[l] + fold(gained)
        shifts[l] = shifts[l] + fold(weight * shift[l : l + 1, :].astype(jnp.float32))
    ones = jnp.ones((16, rows.shape[1]), jnp.bfloat16)
    reads[...] += dot_lanes(jnp.concatenate(gains + [ones], axis=0), rows)
    gram[...] += dot_lanes(rows, rows)
    column[...] += dot_lanes(rows, jnp.ones((128, rows.shape[1]), jnp.bfloat16))


def prepare_kernel(me, grp, kinds, w0, w1, w2, w3, w_env, final, scale, shift, light, *refs):
    partial, (mixer, cross, direct, base, bias), sums = refs[:5], refs[5:10], refs[10:]
    step = pl.program_id(0)
    lights = scale.shape[0]
    width = 2 * pl.num_programs(0) * w0.shape[1]

    @pl.when(step == 0)
    def _():
        for ref, start in zip(sums, partial):
            ref[...] = start[...]

    gather_weights(w0, w1, w2, w3, w_env, final, scale, shift, *sums)
    reads, gram, column, sums, shifts = sums

    @pl.when(step == pl.num_programs(0) - 1)
    def _():
        average = reads[256:257] * (1.0 / width)
        centred = gram[...] * (1.0 / width) - (column[:, :1] * (1.0 / width)) * average
        mixer[:256], mixer[256:512] = split(centred[:256, :256])
        for l in range(lights):
            total = jnp.sum(sums[l], axis=1, keepdims=True)
            read = reads[l * 128 : l * 128 + 64] + reads[l * 128 + 64 : l * 128 + 128]
            read = read - total * average
            start = 512 + l * 128
            mixer[start : start + 64], mixer[start + 64 : start + 128] = split(read[:, :256])
            bias[l] = jnp.broadcast_to(
                jnp.sum(shifts[l], axis=1, keepdims=True), bias.shape[1:]
            )
            tokens = light[l]
            cross[l] = 2.0 * dot_split(centred[:256, 256:], tokens)
            direct[l] = dot_split(read[:, 256:], tokens)
            turned = tokens.astype(jnp.float32).T
            own = jnp.sum(dot_split(centred[256:, 256:], tokens) * turned, axis=0, keepdims=True)
            base[l] = jnp.broadcast_to(own, base.shape[1:])


def render_kernel(place, *refs):
    ready, remote, mean = refs[:4], refs[4:8], refs[8:12]
    mixer, cross, direct, base, bias, attrs, rendered = refs[12:]
    me = place[0]
    found = [
        jnp.concatenate((a[...], blend(r, m)), axis=1) for a, r, m in zip(ready, remote, mean)
    ]
    attrs[pl.ds(me, 1)] = found[0][None]
    attrs[pl.ds(1 - me, 1)] = found[1][None]
    latents = jnp.concatenate(found, axis=0)
    mixed = jnp.dot(mixer[...], latents, preferred_element_type=jnp.float32)
    square = mixed[:256] + mixed[256:512]
    wide = latents.astype(jnp.float32)
    for l in range(rendered.shape[0]):
        spread = jnp.sum(wide * (square + cross[l]), axis=0, keepdims=True) + base[l, :1]
        invert = lax.rsqrt(jnp.maximum(spread, 0.0) + EPS)
        start = 512 + l * 128
        read = mixed[start : start + 64] + mixed[start + 64 : start + 128] + direct[l]
        shift = jnp.concatenate([bias[l]] * (read.shape[1] // 128), axis=1)
        rendered[l] = (read * invert + shift).astype(jnp.bfloat16)


LIMIT = pltpu.CompilerParams(vmem_limit_bytes=14 << 20)
RESIDENT = pl.BlockSpec(memory_space=pltpu.VMEM)


def resident(*arrays):
    return [pltpu.with_memory_space_constraint(a, pltpu.VMEM) for a in arrays]


def stay(array):
    return pltpu.with_memory_space_constraint(array, pltpu.HBM)


def whole(shape):
    return pl.BlockSpec(shape, lambda *_: (0,) * len(shape))


def on_device(
    q_inv,
    k_inv,
    v_inv,
    group_ids,
    w_attr,
    env_ids,
    env_table,
    w_embed_attr,
    w_embed_env,
    mod_scale,
    mod_shift,
    w_final,
):
    groups, rows, width = q_inv.shape
    heads = width // HD
    first = rows // 2
    piece = rows // 4
    patch = w_attr.shape[2]
    lights, model = mod_scale.shape
    channels = w_embed_env.shape[0]
    me = lax.axis_index("seq") % 2
    grp = lax.axis_index("grp")

    place = me.reshape(1).astype(jnp.int32)
    side = grp.reshape(1).astype(jnp.int32)
    scalar = pl.BlockSpec(memory_space=pltpu.SMEM)
    remain = pl.BlockSpec(memory_space=pltpu.HBM)
    ahead, behind = pl.pallas_call(
        first_kernel,
        in_specs=[scalar, remain],
        out_specs=[RESIDENT] * 2,
        out_shape=[pltpu.VMEM((first, width), jnp.bfloat16)] * 2,
        scratch_shapes=[pltpu.SemaphoreType.DMA((2,))],
        compiler_params=LIMIT,
        name="first",
    )(place, stay(q_inv))
    same0 = seq_swap(ahead, 2)
    cross0 = seq_swap(behind, 3)
    bundle, same1, cross1, *late = pl.pallas_call(
        second_kernel,
        in_specs=[scalar, remain, remain, remain],
        out_specs=[remain] * 7,
        out_shape=[pltpu.HBM((3, rows, width), jnp.bfloat16)]
        + [pltpu.HBM((piece, width), jnp.bfloat16)] * 2
        + [pltpu.HBM((piece, width // 2), jnp.bfloat16)] * 4,
        scratch_shapes=[
            pltpu.VMEM((3, rows, width), jnp.bfloat16),
            pltpu.VMEM((4, piece, width), jnp.bfloat16),
        ]
        + [pltpu.SemaphoreType.DMA((9,))] * 2,
        compiler_params=LIMIT,
        name="second",
    )(place, stay(q_inv), stay(k_inv), stay(v_inv))
    bundle = seq_swap(bundle, 1)

    kinds = 4 * patch
    inputs = kinds + channels
    strips = model // CHUNK // 2

    def sweep(start):
        chosen = [
            pl.BlockSpec(
                (None, patch, CHUNK),
                lambda g, m, r, t, n=n: (
                    t[2 * (r[0] if n < 2 else 1 - r[0]) + (1 - m[0] if n % 2 else m[0])],
                    0,
                    g + start,
                ),
            )
            for n in range(4)
        ]
        return chosen + [
            pl.BlockSpec((count, CHUNK), lambda g, *_: (0, g + start))
            for count in (channels, patch, lights, lights)
        ]

    sums = [
        (2 * lights * patch + 16, inputs),
        (inputs, inputs),
        (inputs, 128),
        (lights, patch, 128),
        (lights, patch, 128),
    ]
    weights = (w_embed_attr,) * 4 + (w_embed_env, w_final.T, mod_scale, mod_shift)
    partial = pl.pallas_call(
        begin_kernel,
        grid_spec=pltpu.PrefetchScalarGridSpec(
            num_scalar_prefetch=3,
            grid=(strips,),
            in_specs=sweep(0),
            out_specs=[whole(shape) for shape in sums],
        ),
        out_shape=[jax.ShapeDtypeStruct(shape, jnp.float32) for shape in sums],
        compiler_params=LIMIT,
        name="begin",
    )(place, side, group_ids, *(stay(w) for w in weights))

    cols = STEP_HEADS * HD
    steps = heads // STEP_HEADS
    picked = pl.BlockSpec((None, rows, cols), lambda g, m, *_: (m[0], 0, g))
    given = [
        pl.BlockSpec((None, rows, cols), lambda g, *_, n=n: (n, 0, g)) for n in range(3)
    ]
    reads = pl.BlockSpec((STEP_HEADS, 80, 2 * rows), lambda g, *_: (g, 0, 0))
    vw, mean, mean_own, mean_part, level = pl.pallas_call(
        local_kernel,
        grid_spec=pltpu.PrefetchScalarGridSpec(
            num_scalar_prefetch=3,
            grid=(steps,),
            in_specs=[
                picked,
                given[0],
                picked,
                given[1],
                picked,
                given[2],
                pl.BlockSpec((None, patch, cols), lambda g, m, r, t: (t[2 * r[0] + m[0]], 0, g)),
            ],
            out_specs=[
                reads,
                pl.BlockSpec((STEP_HEADS, 64, rows), lambda g, *_: (g, 0, 0)),
                pl.BlockSpec((STEP_HEADS, 64, first), lambda g, *_: (g, 0, 0)),
                pl.BlockSpec((STEP_HEADS, 64, first), lambda g, *_: (g, 0, 0)),
                whole((heads, 2 * rows)),
            ],
        ),
        out_shape=[
            jax.ShapeDtypeStruct((heads, 80, 2 * rows), jnp.bfloat16),
            jax.ShapeDtypeStruct((heads, 64, rows), jnp.float32),
            jax.ShapeDtypeStruct((heads, 64, first), jnp.bfloat16),
            jax.ShapeDtypeStruct((heads, 64, first), jnp.bfloat16),
            jax.ShapeDtypeStruct((heads, 2 * rows), jnp.float32),
        ],
        compiler_params=LIMIT,
        name="local",
    )(
        place,
        side,
        group_ids,
        stay(q_inv),
        bundle,
        stay(k_inv),
        bundle,
        stay(v_inv),
        bundle,
        stay(jnp.swapaxes(w_attr, 1, 2)),
    )

    level, same1, cross1 = lax.optimization_barrier((level, same1, cross1))
    home = seq_swap(level, 2)
    same1 = seq_swap(same1, 2)
    cross1 = seq_swap(cross1, 3)
    means = [
        mean_own,
        seq_swap(mean_part, 1),
        grp_swap(mean_own),
        both_swap(mean_part, 1),
    ]
    kx = bundle[1]

    lighting = jnp.take(env_table, env_ids, axis=0)
    out_shapes = [
        pltpu.VMEM((2 * kinds + 2 * lights * patch, kinds), jnp.bfloat16),
        pltpu.VMEM((lights, kinds, rows), jnp.float32),
        pltpu.VMEM((lights, patch, rows), jnp.float32),
        pltpu.VMEM((lights, 8, rows), jnp.float32),
        pltpu.VMEM((lights, patch, 128), jnp.float32),
    ]
    prepared = pl.pallas_call(
        prepare_kernel,
        grid_spec=pltpu.PrefetchScalarGridSpec(
            num_scalar_prefetch=3,
            grid=(strips,),
            in_specs=sweep(strips)
            + [whole((lights, rows, channels))]
            + [whole(shape) for shape in sums],
            out_specs=[whole(s.shape) for s in out_shapes],
            scratch_shapes=[pltpu.VMEM(shape, jnp.float32) for shape in sums],
        ),
        out_shape=out_shapes,
        compiler_params=LIMIT,
        name="prepare",
    )(place, side, group_ids, *weights, lighting, *partial)

    def remote(same, crossed, spans, lane):
        count = same.shape[0]
        wide = 2 * count
        block = pl.BlockSpec((count, cols), lambda g, m: (0, g))
        sent = pl.pallas_call(
            lambda *refs: remote_kernel(spans, *refs),
            grid_spec=pltpu.PrefetchScalarGridSpec(
                num_scalar_prefetch=1,
                grid=(steps,),
                in_specs=[
                    block,
                    block,
                    picked,
                    given[1],
                    reads,
                    pl.BlockSpec((heads, wide), lambda g, m: (0, lane)),
                ],
                out_specs=whole((64 + heads, wide)),
                scratch_shapes=[
                    pltpu.VMEM((64, wide), jnp.float32),
                    pltpu.VMEM((heads, wide), jnp.float32),
                ],
            ),
            out_shape=jax.ShapeDtypeStruct((64 + heads, wide), jnp.bfloat16),
            compiler_params=LIMIT,
            name="remote",
        )(place, same, crossed, k_inv, bundle, vw, home)
        return sent

    back0 = remote(same0, cross0, ((0, first),), 0)
    back0, *late = lax.optimization_barrier((back0, *late))
    back0 = seq_swap(back0, 2)
    same2, cross2 = seq_swap(late[0], 2), seq_swap(late[1], 3)
    same3, cross3 = seq_swap(late[2], 2), seq_swap(late[3], 3)

    def attend(stage, same, crossed, *prior):
        last = stage == 2
        shapes = [((64 + heads, first), jnp.bfloat16 if last else jnp.float32)] * (1 + last)
        return pl.pallas_call(
            lambda *refs: last_kernel(stage, *refs),
            in_specs=[scalar] + [RESIDENT] * (6 + stage),
            out_specs=[RESIDENT] * (1 + last),
            out_shape=[pltpu.VMEM(*shape) for shape in shapes],
            scratch_shapes=[
                pltpu.VMEM((64, first), jnp.float32),
                pltpu.VMEM((heads, first), jnp.float32),
                pltpu.VMEM((heads, first), jnp.float32),
            ],
            compiler_params=LIMIT,
            name="last",
        )(place, *resident(same, crossed, k_inv, kx, vw, home, *prior))

    (prior,) = attend(0, same1, cross1)
    own, other = pl.pallas_call(
        join_kernel,
        in_specs=[RESIDENT] * 2,
        out_specs=[RESIDENT] * 2,
        out_shape=[pltpu.VMEM((64, first), jnp.bfloat16)] * 2,
        compiler_params=LIMIT,
        name="join",
    )(*resident(back0, mean))
    ready = [own, seq_swap(other, 1), grp_swap(own), both_swap(other, 1)]
    (half,) = attend(1, same2, cross2, prior)
    sent, passed = attend(2, same3, cross3, prior, half)
    far = [both_swap(sent, 2), both_swap(passed, 3)]
    parts = [seq_swap(sent, 2), seq_swap(passed, 3)] + far
    attrs, rendered = pl.pallas_call(
        render_kernel,
        in_specs=[scalar] + [RESIDENT] * 17,
        out_specs=[RESIDENT] * 2,
        out_shape=[
            jax.ShapeDtypeStruct((groups, patch, rows), jnp.bfloat16),
            jax.ShapeDtypeStruct((lights, patch, rows), jnp.bfloat16),
        ],
        compiler_params=LIMIT,
        name="render",
    )(place, *resident(*ready, *parts, *means, *prepared))
    return (jnp.swapaxes(attrs, 1, 2), jnp.swapaxes(rendered, 1, 2))


def solution(mesh):
    in_specs = (
        P("grp", "seq", None),
        P("grp", "seq", None),
        P("grp", "seq", None),
        P(),
        P(),
        P("grp", "seq"),
        P(),
        P(),
        P(),
        P("grp", None),
        P("grp", None),
        P(),
    )
    out_specs = (P("grp", "seq", None), P("grp", "seq", None))
    return jax.shard_map(
        on_device, mesh=mesh, in_specs=in_specs, out_specs=out_specs, check_vma=False
    )
```

```python
import math

import jax
import jax.numpy as jnp
from jax import lax
from jax.experimental import pallas as pl
from jax.experimental.pallas import tpu as pltpu
from jax.sharding import PartitionSpec as P


HD = 128
STEP_HEADS = 4
EPS = 1e-06
SCALE = HD ** (-0.5) * math.log2(math.e)
SAFE = 60.0
CHUNK = 1024
OVER_LANES = (((1,), (1,)), ((), ()))


def seq_swap(block, flip):
    count = lax.axis_size("seq")
    return lax.ppermute(block, "seq", [(i, i ^ flip) for i in range(count)])


def grp_swap(block):
    return lax.ppermute(block, "grp", [(0, 1), (1, 0)])


def both_swap(block, flip):
    count = lax.axis_size("seq")
    route = [
        (g * count + i, (1 - g) * count + (i ^ flip)) for g in range(2) for i in range(count)
    ]
    return lax.ppermute(block, ("grp", "seq"), route)


def dot_lanes(left, right):
    return lax.dot_general(left, right, OVER_LANES, preferred_element_type=jnp.float32)


def split(block):
    high = block.astype(jnp.bfloat16)
    return high, (block - high.astype(jnp.float32)).astype(jnp.bfloat16)


def dot_split(left, right):
    high, low = split(left)
    return dot_lanes(high, right) + dot_lanes(low, right)


def scores_of(keys, queries):
    half = keys.shape[0] // 2
    return [dot_lanes(keys[:half], queries), dot_lanes(keys[half:], queries)]


def plain_softmax(units):
    found = []
    ahead = scores_of(*units[0][:2])
    for n, (_, _, values) in enumerate(units):
        scores = ahead
        if n + 1 < len(units):
            ahead = scores_of(*units[n + 1][:2])
        half = values.shape[1] // 2
        powers = [jnp.exp2(s * SCALE).astype(jnp.bfloat16) for s in scores]
        summed = jnp.dot(
            values[:, :half], powers[0], preferred_element_type=jnp.float32
        ) + jnp.dot(values[:, half:], powers[1], preferred_element_type=jnp.float32)
        total = summed[64:65]
        found.append((summed[:64], total, jnp.log2(total)))
    return found


def shifted_softmax(units):
    found = []
    for keys, queries, values in units:
        scores = dot_lanes(keys, queries)
        top = jnp.max(scores, axis=0, keepdims=True)
        powers = jnp.exp2((scores - top) * SCALE).astype(jnp.bfloat16)
        summed = jnp.dot(values, powers, preferred_element_type=jnp.float32)
        total = summed[64:65]
        found.append((summed[:64], total, top * SCALE + jnp.log2(total)))
    return found


def worst(levels):
    largest = jnp.abs(levels[0])
    for level in levels[1:]:
        largest = jnp.maximum(largest, jnp.abs(level))
    return jnp.max(largest)


def shuttle(pieces, arrive, leave):
    inward = [
        pltpu.make_async_copy(source, held, arrive.at[n])
        for n, (source, held, _) in enumerate(pieces)
    ]
    outward = [
        pltpu.make_async_copy(held, target, leave.at[n])
        for n, (_, held, target) in enumerate(pieces)
    ]
    for copy in inward:
        copy.start()
    for here, there in zip(inward, outward):
        here.wait()
        there.start()
    for copy in outward:
        copy.wait()


def first_kernel(other, place, q, out, arrive):
    group = 1 - place[0] if other else place[0]
    half = out.shape[0] // 2
    copies = []
    for n in range(2):
        rows = pl.ds(n * half, half)
        copies.append(pltpu.make_async_copy(q.at[group, rows], out.at[rows], arrive.at[n]))
    for copy in copies:
        copy.start()
    for copy in copies:
        copy.wait()


def second_kernel(place, q, k, v, bundle, sb, cb, s1, c1, s2, c2, held, rest, arrive, leave):
    me = place[0]
    count, width = sb.shape
    start = q.shape[1] - 2 * count
    ahead = s1.shape[1]
    left, right = pl.ds(0, ahead), pl.ds(ahead, width - ahead)
    pieces = [(a.at[1 - me], held.at[n], bundle.at[n]) for n, a in enumerate((q, k, v))]
    for n, group, same, first, later in ((0, me, sb, s1, s2), (1, 1 - me, cb, c1, c2)):
        span = pl.ds(start, count)
        pieces.append((q.at[group, span], rest.at[n], same))
        span = pl.ds(start + count, count)
        for cols, target in ((left, first), (right, later)):
            pieces.append((q.at[group, span, cols], rest.at[2 + n, :, cols], target))
    shuttle(pieces, arrive, leave)


def local_kernel(me, grp, kinds, q, qx, k, kx, v, vx, w, vw, mean, own, part, level):
    step = pl.program_id(0)
    reads = []

    for i in range(STEP_HEADS):
        cols = slice(i * HD, (i + 1) * HD)
        values = jnp.concatenate((v[:, cols], vx[:, cols]), axis=0)
        read = dot_lanes(w[:, cols], values).astype(jnp.bfloat16)
        read = jnp.concatenate((read, jnp.ones((16, read.shape[1]), jnp.bfloat16)), axis=0)
        vw[i] = read
        reads.append(read)

    def attend(softmax):
        units = []
        for i in range(STEP_HEADS):
            cols = slice(i * HD, (i + 1) * HD)
            keys = jnp.concatenate((k[:, cols], kx[:, cols]), axis=0)
            for a, b in ((0, 128), (128, 256)):
                queries = jnp.concatenate((q[a:b, cols], qx[a:b, cols]), axis=0)
                units.append((keys, queries, reads[i]))
        found = softmax(units)
        levels = []
        for i in range(STEP_HEADS):
            rows = []
            for n in range(2):
                summed, total, row = found[2 * i + n]
                scaled = summed * (1.0 / total)
                if n == 0:
                    mean[i] = scaled
                else:
                    own[i] = scaled[:, :128].astype(jnp.bfloat16)
                    part[i] = scaled[:, 128:].astype(jnp.bfloat16)
                rows.append(row)
            levels.append(jnp.concatenate(rows, axis=1))
            level[pl.ds(step * STEP_HEADS + i, 1), :] = levels[-1]
        return worst(levels)

    reach = attend(plain_softmax)

    @pl.when(jnp.logical_not(reach < SAFE))
    def _():
        attend(shifted_softmax)


def remote_kernel(spans, me, qs, qd, k, kx, vw, home, out, acc, share):
    step = pl.program_id(0)

    @pl.when(step == 0)
    def _():
        acc[...] = jnp.zeros_like(acc)

    before = acc[...]

    def attend(softmax):
        gathered = [before[:, a * 2 : b * 2] for a, b in spans]
        units = []
        for i in range(STEP_HEADS):
            cols = slice(i * HD, (i + 1) * HD)
            keys = jnp.concatenate((k[:, cols], kx[:, cols]), axis=0)
            for a, b in spans:
                queries = jnp.concatenate((qs[a:b, cols], qd[a:b, cols]), axis=0)
                units.append((keys, queries, vw[i]))
        found = softmax(units)
        levels = []
        for i in range(STEP_HEADS):
            row = pl.ds(step * STEP_HEADS + i, 1)
            theirs = home[row, :]
            rows, mines = [], []
            for n, (a, b) in enumerate(spans):
                summed, total, level = found[i * len(spans) + n]
                mine = 1.0 / (1.0 + jnp.exp2(theirs[:, 2 * a : 2 * b] - level))
                mine = mine.astype(jnp.bfloat16).astype(jnp.float32)
                gathered[n] = gathered[n] + summed * (mine / total)
                mines.append(mine)
                rows.append(level)
            share[row, :] = jnp.concatenate(mines, axis=1)
            levels.append(jnp.concatenate(rows, axis=1))
        for n, (a, b) in enumerate(spans):
            acc[:, 2 * a : 2 * b] = gathered[n]
        return worst(levels)

    reach = attend(plain_softmax)

    @pl.when(jnp.logical_not(reach < SAFE))
    def _():
        attend(shifted_softmax)

    @pl.when(step == pl.num_programs(0) - 1)
    def _():
        out[:64] = acc[...].astype(jnp.bfloat16)
        out[64:] = share[...].astype(jnp.bfloat16)


def halves(left, right):
    first = lax.broadcasted_iota(jnp.int32, left.shape, 1) < 64
    return (
        jnp.where(first, left, pltpu.roll(right, 64, 1)),
        jnp.where(first, pltpu.roll(left, 64, 1), right),
    )


def last_kernel(stage, place, qs, qd, k, kx, vw, home, *refs):
    prior, outs, (acc, share, near) = refs[:stage], refs[stage:-3], refs[-3:]
    me = place[0]
    base = vw.shape[0] - qs.shape[1] // HD if stage == 2 else 0
    heads = base + qs.shape[1] // HD
    near[...] = halves(home[:, 256:384], home[:, 384:512])[1 if stage else 0]
    zero = jnp.zeros((2 * qs.shape[0], HD), jnp.bfloat16)
    if stage == 2:
        seed = prior[1][:64]
        share[:base] = prior[1][64 : 64 + base]
    else:
        seed = jnp.zeros(acc.shape, jnp.float32)

    def scores_at(head):
        cols = pl.ds(head * HD, 2 * HD)
        near_cols = pl.ds((head - base) * HD, 2 * HD)
        if not isinstance(head, int):
            cols = pl.ds(pl.multiple_of(head * HD, 2 * HD), 2 * HD)
            near_cols = pl.ds(pl.multiple_of((head - base) * HD, 2 * HD), 2 * HD)
        keys = jnp.concatenate((k[me, :, cols], kx[:, cols]), axis=0)
        pair = jnp.concatenate((qs[:, near_cols], qd[:, near_cols]), axis=0)
        queries = jnp.concatenate(
            (
                jnp.concatenate((pair[:, :HD], zero), axis=1),
                jnp.concatenate((zero, pair[:, HD:]), axis=1),
            ),
            axis=0,
        )
        half = keys.shape[0] // 2
        return [dot_lanes(keys[:half], queries), dot_lanes(keys[half:], queries)]

    def finish(head, scores, top):
        wide = scores[0].shape[1] // 2
        powers = []
        for block in scores:
            shifted = block if top is None else block - top
            powers.append(jnp.exp2(shifted * SCALE).astype(jnp.bfloat16))
        found = []
        for n in range(2):
            read = vw[head + n]
            half = read.shape[1] // 2
            lanes = slice(n * wide, (n + 1) * wide)
            summed = jnp.dot(
                read[:, :half], powers[0][:, lanes], preferred_element_type=jnp.float32
            ) + jnp.dot(read[:, half:], powers[1][:, lanes], preferred_element_type=jnp.float32)
            total = summed[64:65]
            level = jnp.log2(total)
            if top is not None:
                level = level + top[:, lanes] * SCALE
            row = pl.ds(head + n, 1)
            mine = 1.0 / (1.0 + jnp.exp2(near[row, :] - level))
            mine = mine.astype(jnp.bfloat16).astype(jnp.float32)
            share[row, :] = mine
            found.append((summed[:64] * (mine / total), level))
        return found

    gathered = seed
    levels = []
    ahead = scores_at(base)
    for head in range(base, heads, 2):
        scores = ahead
        if head + 2 < heads:
            ahead = scores_at(head + 2)
        for piece, level in finish(head, scores, None):
            gathered = gathered + piece
            levels.append(level)
    acc[...] = gathered

    @pl.when(jnp.logical_not(worst(levels) < SAFE))
    def _():
        acc[...] = seed

        def body(n, carry):
            scores = scores_at(base + 2 * n)
            top = jnp.maximum(*(jnp.max(s, axis=0, keepdims=True) for s in scores))
            for piece, _ in finish(base + 2 * n, scores, top):
                acc[...] += piece
            return carry

        lax.fori_loop(0, (heads - base) // 2, body, 0)

    if stage < 2:
        outs[0][:64] = acc[...]
        outs[0][64 : 64 + heads] = share[:heads]
    else:
        for a, b, now in ((0, 64, acc), (64, 64 + heads, share)):
            own, part = halves(prior[0][a:b], now[...])
            outs[0][a:b] = own.astype(jnp.bfloat16)
            outs[1][a:b] = part.astype(jnp.bfloat16)


def blend(remote, mean):
    acc = remote[:64].astype(jnp.float32)
    for h in range(mean.shape[0]):
        keep = 1.0 - remote[64 + h : 65 + h].astype(jnp.float32)
        acc = acc + mean[h].astype(jnp.float32) * keep
    return acc.astype(jnp.bfloat16)


def join_kernel(remote, mean, own, other):
    found = blend(remote, mean)
    half = found.shape[1] // 2
    own[...] = found[:, :half]
    other[...] = found[:, half:]


def begin_kernel(me, grp, kinds, w0, w1, w2, w3, w_env, final, scale, shift, *sums):
    @pl.when(pl.program_id(0) == 0)
    def _():
        for ref in sums:
            ref[...] = jnp.zeros_like(ref)

    gather_weights(w0, w1, w2, w3, w_env, final, scale, shift, *sums)


def gather_weights(w0, w1, w2, w3, w_env, final, scale, shift, reads, gram, column, sums, shifts):
    lights = scale.shape[0]
    rows = jnp.concatenate((w0[...], w1[...], w2[...], w3[...], w_env[...]), axis=0)
    weight = final[...].astype(jnp.float32)

    def fold(block):
        total = block[:, :128]
        for s in range(1, block.shape[1] // 128):
            total = total + block[:, s * 128 : (s + 1) * 128]
        return total

    gains = []
    for l in range(lights):
        gained = weight * (1.0 + scale[l : l + 1, :].astype(jnp.float32))
        gains += split(gained)
        sums[l] = sums[l] + fold(gained)
        shifts[l] = shifts[l] + fold(weight * shift[l : l + 1, :].astype(jnp.float32))
    ones = jnp.ones((16, rows.shape[1]), jnp.bfloat16)
    reads[...] += dot_lanes(jnp.concatenate(gains + [ones], axis=0), rows)
    gram[...] += dot_lanes(rows, rows)
    column[...] += dot_lanes(rows, jnp.ones((128, rows.shape[1]), jnp.bfloat16))


def prepare_kernel(me, grp, kinds, w0, w1, w2, w3, w_env, final, scale, shift, light, *refs):
    partial, (mixer, cross, direct, base, bias), sums = refs[:5], refs[5:10], refs[10:]
    step = pl.program_id(0)
    lights = scale.shape[0]
    width = 2 * pl.num_programs(0) * w0.shape[1]

    @pl.when(step == 0)
    def _():
        for ref, start in zip(sums, partial):
            ref[...] = start[...]

    gather_weights(w0, w1, w2, w3, w_env, final, scale, shift, *sums)
    reads, gram, column, sums, shifts = sums

    @pl.when(step == pl.num_programs(0) - 1)
    def _():
        average = reads[256:257] * (1.0 / width)
        centred = gram[...] * (1.0 / width) - (column[:, :1] * (1.0 / width)) * average
        mixer[:256], mixer[256:512] = split(centred[:256, :256])
        for l in range(lights):
            total = jnp.sum(sums[l], axis=1, keepdims=True)
            read = reads[l * 128 : l * 128 + 64] + reads[l * 128 + 64 : l * 128 + 128]
            read = read - total * average
            start = 512 + l * 128
            mixer[start : start + 64], mixer[start + 64 : start + 128] = split(read[:, :256])
            bias[l] = jnp.broadcast_to(
                jnp.sum(shifts[l], axis=1, keepdims=True), bias.shape[1:]
            )
            tokens = light[l]
            cross[l] = 2.0 * dot_split(centred[:256, 256:], tokens)
            direct[l] = dot_split(read[:, 256:], tokens)
            turned = tokens.astype(jnp.float32).T
            own = jnp.sum(dot_split(centred[256:, 256:], tokens) * turned, axis=0, keepdims=True)
            base[l] = jnp.broadcast_to(own, base.shape[1:])


def render_kernel(place, *refs):
    ready, remote, mean = refs[:4], refs[4:8], refs[8:12]
    mixer, cross, direct, base, bias, attrs, rendered = refs[12:]
    me = place[0]
    found = [
        jnp.concatenate((a[...], blend(r, m)), axis=1) for a, r, m in zip(ready, remote, mean)
    ]
    attrs[pl.ds(me, 1)] = found[0][None]
    attrs[pl.ds(1 - me, 1)] = found[1][None]
    latents = jnp.concatenate(found, axis=0)
    mixed = jnp.dot(mixer[...], latents, preferred_element_type=jnp.float32)
    square = mixed[:256] + mixed[256:512]
    wide = latents.astype(jnp.float32)
    for l in range(rendered.shape[0]):
        spread = jnp.sum(wide * (square + cross[l]), axis=0, keepdims=True) + base[l, :1]
        invert = lax.rsqrt(jnp.maximum(spread, 0.0) + EPS)
        start = 512 + l * 128
        read = mixed[start : start + 64] + mixed[start + 64 : start + 128] + direct[l]
        shift = jnp.concatenate([bias[l]] * (read.shape[1] // 128), axis=1)
        rendered[l] = (read * invert + shift).astype(jnp.bfloat16)


LIMIT = pltpu.CompilerParams(vmem_limit_bytes=14 << 20)
RESIDENT = pl.BlockSpec(memory_space=pltpu.VMEM)


def resident(*arrays):
    return [pltpu.with_memory_space_constraint(a, pltpu.VMEM) for a in arrays]


def stay(array):
    return pltpu.with_memory_space_constraint(array, pltpu.HBM)


def whole(shape):
    return pl.BlockSpec(shape, lambda *_: (0,) * len(shape))


def on_device(
    q_inv,
    k_inv,
    v_inv,
    group_ids,
    w_attr,
    env_ids,
    env_table,
    w_embed_attr,
    w_embed_env,
    mod_scale,
    mod_shift,
    w_final,
):
    groups, rows, width = q_inv.shape
    heads = width // HD
    first = rows // 2
    piece = rows // 4
    soon = 3 * heads // 4
    patch = w_attr.shape[2]
    lights, model = mod_scale.shape
    channels = w_embed_env.shape[0]
    me = lax.axis_index("seq") % 2
    grp = lax.axis_index("grp")

    place = me.reshape(1).astype(jnp.int32)
    side = grp.reshape(1).astype(jnp.int32)
    scalar = pl.BlockSpec(memory_space=pltpu.SMEM)
    remain = pl.BlockSpec(memory_space=pltpu.HBM)

    def cut(other):
        return pl.pallas_call(
            lambda *refs: first_kernel(other, *refs),
            in_specs=[scalar, remain],
            out_specs=RESIDENT,
            out_shape=pltpu.VMEM((first, width), jnp.bfloat16),
            scratch_shapes=[pltpu.SemaphoreType.DMA((2,))],
            compiler_params=LIMIT,
            name="first",
        )(place, stay(q_inv))

    ahead = cut(False)
    same0 = seq_swap(ahead, 2)
    behind = cut(True)
    cross0 = seq_swap(behind, 3)
    bundle, same1, cross1, *late = pl.pallas_call(
        second_kernel,
        in_specs=[scalar, remain, remain, remain],
        out_specs=[remain] * 7,
        out_shape=[pltpu.HBM((3, rows, width), jnp.bfloat16)]
        + [pltpu.HBM((piece, width), jnp.bfloat16)] * 2
        + [pltpu.HBM((piece, n * HD), jnp.bfloat16) for n in (soon, heads - soon) for _ in range(2)],
        scratch_shapes=[
            pltpu.VMEM((3, rows, width), jnp.bfloat16),
            pltpu.VMEM((4, piece, width), jnp.bfloat16),
        ]
        + [pltpu.SemaphoreType.DMA((9,))] * 2,
        compiler_params=LIMIT,
        name="second",
    )(place, stay(q_inv), stay(k_inv), stay(v_inv))
    bundle = seq_swap(bundle, 1)

    kinds = 4 * patch
    inputs = kinds + channels
    strips = model // CHUNK // 2

    def sweep(start):
        chosen = [
            pl.BlockSpec(
                (None, patch, CHUNK),
                lambda g, m, r, t, n=n: (
                    t[2 * (r[0] if n < 2 else 1 - r[0]) + (1 - m[0] if n % 2 else m[0])],
                    0,
                    g + start,
                ),
            )
            for n in range(4)
        ]
        return chosen + [
            pl.BlockSpec((count, CHUNK), lambda g, *_: (0, g + start))
            for count in (channels, patch, lights, lights)
        ]

    sums = [
        (2 * lights * patch + 16, inputs),
        (inputs, inputs),
        (inputs, 128),
        (lights, patch, 128),
        (lights, patch, 128),
    ]
    weights = (w_embed_attr,) * 4 + (w_embed_env, w_final.T, mod_scale, mod_shift)
    partial = pl.pallas_call(
        begin_kernel,
        grid_spec=pltpu.PrefetchScalarGridSpec(
            num_scalar_prefetch=3,
            grid=(strips,),
            in_specs=sweep(0),
            out_specs=[whole(shape) for shape in sums],
        ),
        out_shape=[jax.ShapeDtypeStruct(shape, jnp.float32) for shape in sums],
        compiler_params=LIMIT,
        name="begin",
    )(place, side, group_ids, *(stay(w) for w in weights))

    cols = STEP_HEADS * HD
    steps = heads // STEP_HEADS
    picked = pl.BlockSpec((None, rows, cols), lambda g, m, *_: (m[0], 0, g))
    given = [
        pl.BlockSpec((None, rows, cols), lambda g, *_, n=n: (n, 0, g)) for n in range(3)
    ]
    reads = pl.BlockSpec((STEP_HEADS, 80, 2 * rows), lambda g, *_: (g, 0, 0))
    vw, mean, mean_own, mean_part, level = pl.pallas_call(
        local_kernel,
        grid_spec=pltpu.PrefetchScalarGridSpec(
            num_scalar_prefetch=3,
            grid=(steps,),
            in_specs=[
                picked,
                given[0],
                picked,
                given[1],
                picked,
                given[2],
                pl.BlockSpec((None, patch, cols), lambda g, m, r, t: (t[2 * r[0] + m[0]], 0, g)),
            ],
            out_specs=[
                reads,
                pl.BlockSpec((STEP_HEADS, 64, rows), lambda g, *_: (g, 0, 0)),
                pl.BlockSpec((STEP_HEADS, 64, first), lambda g, *_: (g, 0, 0)),
                pl.BlockSpec((STEP_HEADS, 64, first), lambda g, *_: (g, 0, 0)),
                whole((heads, 2 * rows)),
            ],
        ),
        out_shape=[
            jax.ShapeDtypeStruct((heads, 80, 2 * rows), jnp.bfloat16),
            jax.ShapeDtypeStruct((heads, 64, rows), jnp.float32),
            jax.ShapeDtypeStruct((heads, 64, first), jnp.bfloat16),
            jax.ShapeDtypeStruct((heads, 64, first), jnp.bfloat16),
            jax.ShapeDtypeStruct((heads, 2 * rows), jnp.float32),
        ],
        compiler_params=LIMIT,
        name="local",
    )(
        place,
        side,
        group_ids,
        stay(q_inv),
        bundle,
        stay(k_inv),
        bundle,
        stay(v_inv),
        bundle,
        stay(jnp.swapaxes(w_attr, 1, 2)),
    )

    level, same1, cross1 = lax.optimization_barrier((level, same1, cross1))
    home = seq_swap(level, 2)
    same1 = seq_swap(same1, 2)
    cross1 = seq_swap(cross1, 3)
    means = [
        mean_own,
        seq_swap(mean_part, 1),
        grp_swap(mean_own),
        both_swap(mean_part, 1),
    ]
    kx = bundle[1]

    lighting = jnp.take(env_table, env_ids, axis=0)
    out_shapes = [
        pltpu.VMEM((2 * kinds + 2 * lights * patch, kinds), jnp.bfloat16),
        pltpu.VMEM((lights, kinds, rows), jnp.float32),
        pltpu.VMEM((lights, patch, rows), jnp.float32),
        pltpu.VMEM((lights, 8, rows), jnp.float32),
        pltpu.VMEM((lights, patch, 128), jnp.float32),
    ]
    prepared = pl.pallas_call(
        prepare_kernel,
        grid_spec=pltpu.PrefetchScalarGridSpec(
            num_scalar_prefetch=3,
            grid=(strips,),
            in_specs=sweep(strips)
            + [whole((lights, rows, channels))]
            + [whole(shape) for shape in sums],
            out_specs=[whole(s.shape) for s in out_shapes],
            scratch_shapes=[pltpu.VMEM(shape, jnp.float32) for shape in sums],
        ),
        out_shape=out_shapes,
        compiler_params=LIMIT,
        name="prepare",
    )(place, side, group_ids, *weights, lighting, *partial)

    def remote(same, crossed, spans, lane):
        count = same.shape[0]
        wide = 2 * count
        block = pl.BlockSpec((count, cols), lambda g, m: (0, g))
        sent = pl.pallas_call(
            lambda *refs: remote_kernel(spans, *refs),
            grid_spec=pltpu.PrefetchScalarGridSpec(
                num_scalar_prefetch=1,
                grid=(steps,),
                in_specs=[
                    block,
                    block,
                    picked,
                    given[1],
                    reads,
                    pl.BlockSpec((heads, wide), lambda g, m: (0, lane)),
                ],
                out_specs=whole((64 + heads, wide)),
                scratch_shapes=[
                    pltpu.VMEM((64, wide), jnp.float32),
                    pltpu.VMEM((heads, wide), jnp.float32),
                ],
            ),
            out_shape=jax.ShapeDtypeStruct((64 + heads, wide), jnp.bfloat16),
            compiler_params=LIMIT,
            name="remote",
        )(place, same, crossed, k_inv, bundle, vw, home)
        return sent

    back0 = remote(same0, cross0, ((0, first),), 0)
    back0, *late = lax.optimization_barrier((back0, *late))
    back0 = seq_swap(back0, 2)
    same2, cross2 = seq_swap(late[0], 2), seq_swap(late[1], 3)
    same3, cross3 = seq_swap(late[2], 2), seq_swap(late[3], 3)

    def attend(stage, same, crossed, *prior):
        last = stage == 2
        shapes = [((64 + heads, first), jnp.bfloat16 if last else jnp.float32)] * (1 + last)
        return pl.pallas_call(
            lambda *refs: last_kernel(stage, *refs),
            in_specs=[scalar] + [RESIDENT] * (6 + stage),
            out_specs=[RESIDENT] * (1 + last),
            out_shape=[pltpu.VMEM(*shape) for shape in shapes],
            scratch_shapes=[
                pltpu.VMEM((64, first), jnp.float32),
                pltpu.VMEM((heads, first), jnp.float32),
                pltpu.VMEM((heads, first), jnp.float32),
            ],
            compiler_params=LIMIT,
            name="last",
        )(place, *resident(same, crossed, k_inv, kx, vw, home, *prior))

    (prior,) = attend(0, same1, cross1)
    own, other = pl.pallas_call(
        join_kernel,
        in_specs=[RESIDENT] * 2,
        out_specs=[RESIDENT] * 2,
        out_shape=[pltpu.VMEM((64, first), jnp.bfloat16)] * 2,
        compiler_params=LIMIT,
        name="join",
    )(*resident(back0, mean))
    ready = [own, seq_swap(other, 1), grp_swap(own), both_swap(other, 1)]
    (half,) = attend(1, same2, cross2, prior)
    sent, passed = attend(2, same3, cross3, prior, half)
    far = [both_swap(sent, 2), both_swap(passed, 3)]
    parts = [seq_swap(sent, 2), seq_swap(passed, 3)] + far
    attrs, rendered = pl.pallas_call(
        render_kernel,
        in_specs=[scalar] + [RESIDENT] * 17,
        out_specs=[RESIDENT] * 2,
        out_shape=[
            jax.ShapeDtypeStruct((groups, patch, rows), jnp.bfloat16),
            jax.ShapeDtypeStruct((lights, patch, rows), jnp.bfloat16),
        ],
        compiler_params=LIMIT,
        name="render",
    )(place, *resident(*ready, *parts, *means, *prepared))
    return (jnp.swapaxes(attrs, 1, 2), jnp.swapaxes(rendered, 1, 2))


def solution(mesh):
    in_specs = (
        P("grp", "seq", None),
        P("grp", "seq", None),
        P("grp", "seq", None),
        P(),
        P(),
        P("grp", "seq"),
        P(),
        P(),
        P(),
        P("grp", None),
        P("grp", None),
        P(),
    )
    out_specs = (P("grp", "seq", None), P("grp", "seq", None))
    return jax.shard_map(
        on_device, mesh=mesh, in_specs=in_specs, out_specs=out_specs, check_vma=False
    )
```
